32 devices in a mesh: groups: 2 (over x), tensor: 16 (over z, y, core).
Axes of the slice: x: 2, y: 2, z: 4, core: 2. Of those that a mesh axis runs over, the one named last changes fastest.
Arguments:
- span_rows: bfloat16 [32, 8192], P(('groups', 'tensor')), parts along dimension 0, may hold values from -6 to 6
- decode_rows: bfloat16 [2, 32, 8192], P(None, ('groups', 'tensor')), parts along dimension 1, may hold values from -6 to 6
- norm_gain: bfloat16 [8192], replicated, may hold values from 0.099609375 to 1.8984375
- w_query: bfloat16 [8192, 8192], P(None, 'tensor'), may hold values from -0.0625 to 0.0625
- w_keyval: bfloat16 [8192, 2048], P(None, 'tensor'), may hold values from -0.0625 to 0.0625
- prefix_keys: bfloat16 [8192, 1024], P(('groups', 'tensor')), parts along dimension 0, may hold values from -304 to 304
- prefix_values: bfloat16 [8192, 1024], P(('groups', 'tensor')), parts along dimension 0, may hold values from -6 to 6
- span_offset: int32 [2], P('groups'), parts along dimension 0, may hold values from 2048 to 4096
- pool_keys: bfloat16 [1024, 16, 1024], P(('groups', 'tensor')), parts along dimension 0, may hold values from -304 to 304
- pool_values: bfloat16 [1024, 16, 1024], P(('groups', 'tensor')), parts along dimension 0, may hold values from -6 to 6
- row_blocks: int32 [32, 32], P('groups'), parts along dimension 0, may hold values from 0 to 511, as said below
- context_lens: int32 [32], P('groups'), parts along dimension 0, may hold values from 1 to 512, 4096 in all
Outputs:
- span_attended: bfloat16 [32, 8192], P(('groups', 'tensor')), parts along dimension 0
- decode_attended: bfloat16 [2, 32, 8192], P(None, ('groups', 'tensor')), parts along dimension 1
- span_cache: bfloat16 [32, 2048], P(('groups', 'tensor')), parts along dimension 0
The draws below stay inside these ranges and needn't reach their ends.
There are 2 independent parts, one for each index of `groups`. The reference program is written for one: setup_inputs(seed, part) draws one part's arguments, and reference() takes and returns one part's arrays. A program takes and returns all parts, laid end to end along the dimension named above; an argument that names none is the same for every part. Nothing has to cross between parts.
Inputs may be any that keep to these rules, and one draw needn't show every extreme that they name: Prefix slots from span_offset on are unused. `row_blocks`: every cache block belongs to exactly one decode row; entry k of a row holds its positions k * 16 to k * 16 + 15. `context_lens`: some row has exactly 512 cached tokens.
All inputs are finite; a program needn't handle non-finite values.
Results may differ from the reference program's by a relative error of at most 0.0065.
The reference program's roundings to bfloat16 on the way count: a program that leaves them out, or rounds other values in their place, can miss the bound.
Values may be sent and summed in bfloat16 or wider, within the bound.
A program may use at most 128 MiB of HBM per device.

```python
import math
import jax
import jax.numpy as jnp
import numpy as np
from jax import lax

D = 8192
H = 64
KVH = 8
HD = 128
PAGE = 16
STEPS = 2
SPAN = 16
ROWS = 16
PREFIX = 4096
BLOCKS = 512
BLK_ROW = 32


def block_order(key):
    return jax.random.permutation(jax.random.fold_in(key, 11), BLOCKS).astype(jnp.int32).reshape(ROWS, BLK_ROW)


def draw_row_blocks(key, part):
    return block_order(key)


def draw_prefix_keys(key, part):
    key_width = KVH * HD
    drawn = jnp.clip(jax.random.normal(jax.random.fold_in(key, 5), (PREFIX, key_width), jnp.float32), -6.0, 6.0)
    return drawn.astype(jnp.bfloat16)


def draw_pool_keys(key, part):
    key_width = KVH * HD
    drawn = jnp.clip(jax.random.normal(jax.random.fold_in(key, 19), (BLOCKS, PAGE, key_width), jnp.float32), -6.0, 6.0)
    return drawn.astype(jnp.bfloat16)


def block_levels(rng, dims, cuts, smallest, largest):
    gain, own = 1.0, jax.random.fold_in(rng, 6)
    for position, parts in cuts:
        draws = jnp.exp(jax.random.uniform(jax.random.fold_in(own, position), (parts,), jnp.float32, smallest / len(cuts), largest / len(cuts)))
        gain = gain * jnp.repeat(draws, dims[position] // parts).reshape([-1 if axis == position else 1 for axis in range(len(dims))])
    return gain


def split_up(number_of, total, most, lean):
    weights = [(1 << 20) // math.isqrt(grade ** lean) + 1 for grade in range(2, number_of + 1)]
    surplus, counts = total - most - (number_of - 1), [1] * (number_of - 1)
    while surplus > 0:
        free = [i for i in range(number_of - 1) if counts[i] < most]
        whole, budget = sum([weights[i] for i in free]), surplus
        for i in free:
            more = min(most - counts[i], max(1, budget * weights[i] // whole), surplus)
            counts[i] = counts[i] + more
            surplus = surplus - more
    return np.array([most] + counts)


def ragged(rng, amount, total, bound, slope):
    if amount == 2:
        one = jax.random.randint(rng, (), max(1, total - bound), min(bound, total - 1) + 1)
        return jnp.stack([one, total - one])
    sizes = jnp.asarray(split_up(amount, total, bound, slope), jnp.int32)
    twos = (amount - 1) // 2
    source_of, taker = sizes[1:1 + 2 * twos:2], sizes[2:2 + 2 * twos:2]
    margin = jnp.minimum(source_of - 1, bound - taker)
    shifted = jax.random.randint(jax.random.fold_in(rng, 1), (twos,), 0, 1 << 20) % (margin + 1)
    sizes = sizes.at[1:1 + 2 * twos:2].set(source_of - shifted).at[2:2 + 2 * twos:2].set(taker + shifted)
    return sizes[jax.random.permutation(jax.random.fold_in(rng, 2), amount)]


def noise(stream_key, dims, spread, reach, split=(), held_as=jnp.bfloat16):
    gain = block_levels(stream_key, dims, split, -0.22, 0.18) if split else 1.0
    entries = jax.random.normal(stream_key, dims, jnp.float32) * spread * gain
    return jnp.minimum(jnp.maximum(entries, -reach), reach).astype(held_as)


def setup_inputs(seed: int = 0, part: int = 0) -> dict:
    keys = jax.random.split(jax.random.key(seed), 13)
    own_keys = jax.random.split(jax.random.fold_in(keys[12], part), 13)
    span_rows = noise(own_keys[0], (SPAN, D), 1.0, 6.0, ((0, 16),))
    decode_rows = noise(own_keys[1], (STEPS, ROWS, D), 1.0, 6.0, ((1, 16),))
    norm_gain = jnp.clip(1.0 + 0.18 * jax.random.normal(keys[2], (D,), jnp.float32), 0.099609375, 1.8984375).astype(jnp.bfloat16)
    w_query = noise(keys[3], (D, D), D ** -0.5, 0.0625, ((1, 16),))
    w_keyval = noise(keys[4], (D, 2 * KVH * HD), D ** -0.5, 0.0625, ((1, 16),))
    prefix_keys = draw_prefix_keys(jax.random.fold_in(jax.random.fold_in(keys[12], part), 71), part)
    prefix_values = noise(own_keys[6], (PREFIX, KVH * HD), 1.0, 6.0, ((0, 16),))
    span_offset = jax.random.randint(own_keys[7], (1,), PREFIX // 2, PREFIX + 1).astype(jnp.int32)
    pool_keys = draw_pool_keys(jax.random.fold_in(jax.random.fold_in(keys[12], part), 71), part)
    pool_values = noise(own_keys[9], (BLOCKS, PAGE, KVH * HD), 1.0, 6.0, ((0, 16),))
    row_blocks = draw_row_blocks(jax.random.fold_in(jax.random.fold_in(keys[12], part), 71), part)
    context_lens = ragged(own_keys[11], ROWS, ROWS * BLK_ROW * PAGE // 2, BLK_ROW * PAGE, 2).astype(jnp.int32)
    return dict(span_rows=span_rows, decode_rows=decode_rows, norm_gain=norm_gain, w_query=w_query, w_keyval=w_keyval, prefix_keys=prefix_keys, prefix_values=prefix_values, span_offset=span_offset, pool_keys=pool_keys, pool_values=pool_values, row_blocks=row_blocks, context_lens=context_lens)


epsilon = 1e-05
neg_fill = -1e+30
rotation_bits = 20

def normalize(row_block, gain_vector):
    widened = row_block.astype(jnp.float32)
    mean_square = lax.optimization_barrier(jnp.mean(widened * widened, axis=-1, keepdims=True))
    return (widened * lax.rsqrt(mean_square + epsilon) * gain_vector.astype(jnp.float32)).astype(jnp.bfloat16)

def llama_frequencies(half_width):
    exponents = np.arange(half_width) / (1.0 * half_width)
    inverse = 1.0 / 500000.0 ** exponents
    wavelen = 2.0 * np.pi / inverse
    scaled = np.where(wavelen > 8192.0, inverse / 8.0, inverse)
    smooth = (8192.0 / wavelen - 1.0) / 3.0
    blended = (1.0 - smooth) * inverse / 8.0 + smooth * inverse
    middle = (wavelen >= 2048.0) & (wavelen <= 8192.0)
    return np.where(middle, blended, scaled)

def rotation_tables(half_width):
    frequencies = llama_frequencies(half_width)
    powers = 2.0 ** np.arange(rotation_bits)
    angles = powers[:, None] * frequencies[None, :]
    return (jnp.asarray(np.cos(angles), jnp.float32), jnp.asarray(np.sin(angles), jnp.float32))

def rotate(projected, positions, head_count):
    row_count = projected.shape[0]
    half_width = HD // 2
    cos_table, sin_table = rotation_tables(half_width)
    cos_part = jnp.ones((row_count, half_width), jnp.float32)
    sin_part = jnp.zeros((row_count, half_width), jnp.float32)
    for bit_index in range(rotation_bits):
        chosen = (positions >> bit_index & 1).astype(jnp.float32)[:, None]
        step_cos = 1.0 + chosen * (cos_table[bit_index] - 1.0)
        step_sin = chosen * sin_table[bit_index]
        cos_part, sin_part = (cos_part * step_cos - sin_part * step_sin, sin_part * step_cos + cos_part * step_sin)
    shaped = projected.astype(jnp.float32).reshape(row_count, head_count, HD)
    first_half = shaped[..., :half_width]
    second_half = shaped[..., half_width:]
    cos_part = cos_part[:, None, :]
    sin_part = sin_part[:, None, :]
    turned = jnp.concatenate([first_half * cos_part - second_half * sin_part, second_half * cos_part + first_half * sin_part], axis=-1)
    return turned.reshape(row_count, head_count * HD).astype(jnp.bfloat16)

def soft_attend(queries, key_rows, value_rows, allowed, score_scale, form_scores, form_values):
    scores = jnp.einsum(form_scores, queries, key_rows) * score_scale
    scores = jnp.where(allowed, scores, neg_fill)
    row_max = lax.optimization_barrier(jnp.max(scores, axis=-1, keepdims=True))
    weights = jnp.where(allowed, jnp.exp(scores - row_max), 0.0)
    weight_sum = lax.optimization_barrier(jnp.sum(weights, axis=-1))
    rounded = lax.optimization_barrier(weights.astype(jnp.bfloat16)).astype(jnp.float32)
    numerator = jnp.einsum(form_values, rounded, value_rows)
    return (numerator / weight_sum[..., None]).astype(jnp.bfloat16)

def reference(span_rows, decode_rows, norm_gain, w_query, w_keyval, prefix_keys, prefix_values, span_offset, pool_keys, pool_values, row_blocks, context_lens):
    group_size = H // KVH
    kv_width = KVH * HD
    score_scale = 1.0 / math.sqrt(HD)
    offset = span_offset[0]

    def project(normed):
        queries = jnp.dot(normed, w_query, preferred_element_type=jnp.float32).astype(jnp.bfloat16)
        keyval = jnp.dot(normed, w_keyval, preferred_element_type=jnp.float32).astype(jnp.bfloat16)
        return (queries, keyval)
    span_queries, span_keyval = project(normalize(span_rows, norm_gain))
    decode_queries, decode_keyval = project(normalize(decode_rows.reshape(STEPS * ROWS, D), norm_gain))
    span_positions = offset + jnp.arange(SPAN, dtype=jnp.int32)
    decode_positions = (context_lens[None, :] + jnp.arange(STEPS, dtype=jnp.int32)[:, None]).reshape(-1)
    span_queries = rotate(span_queries, span_positions, H)
    span_keys = rotate(span_keyval[:, :kv_width], span_positions, KVH)
    span_values = span_keyval[:, kv_width:]
    decode_queries = rotate(decode_queries, decode_positions, H).reshape(STEPS, ROWS, D)
    decode_keys = rotate(decode_keyval[:, :kv_width], decode_positions, KVH).reshape(STEPS, ROWS, kv_width)
    decode_values = decode_keyval[:, kv_width:].reshape(STEPS, ROWS, kv_width)
    span_cache = jnp.concatenate([span_keys, span_values], axis=1)
    key_count = PREFIX + SPAN
    keys_by_head = jnp.concatenate([prefix_keys, span_keys], axis=0).reshape(key_count, KVH, HD).transpose(1, 0, 2)
    values_by_head = jnp.concatenate([prefix_values, span_values], axis=0).reshape(key_count, KVH, HD).transpose(1, 0, 2)
    query_block = min(SPAN, 16)
    block_count = SPAN // query_block
    queries_by_head = span_queries.reshape(SPAN, KVH, group_size, HD).transpose(1, 0, 2, 3)
    key_index = jnp.arange(key_count, dtype=jnp.int32)
    query_index = jnp.arange(SPAN, dtype=jnp.int32).reshape(block_count, query_block)

    def per_head(packed):
        head_queries, head_keys, head_values = packed
        keys_wide = head_keys.astype(jnp.float32)
        values_wide = head_values.astype(jnp.float32)

        def per_block(inner):
            block_queries, block_index = inner
            allowed = jnp.where(key_index[None, :] < PREFIX, key_index[None, :] < offset, key_index[None, :] - PREFIX <= block_index[:, None])
            return soft_attend(block_queries.astype(jnp.float32), keys_wide, values_wide, allowed[:, None, :], score_scale, 'iqd,kd->iqk', 'iqk,kd->iqd')
        return lax.map(per_block, (head_queries.reshape(block_count, query_block, group_size, HD), query_index))
    results = lax.map(per_head, (queries_by_head, keys_by_head, values_by_head))
    span_attended = results.reshape(KVH, SPAN, group_size, HD).transpose(1, 0, 2, 3).reshape(SPAN, D)
    context = BLK_ROW * PAGE
    seen_index = jnp.arange(context + STEPS, dtype=jnp.int32)
    step_index = jnp.arange(STEPS, dtype=jnp.int32)

    def per_row(packed):
        blocks, length, row_queries, new_keys, new_values = packed
        row_keys = jnp.take(pool_keys, blocks, axis=0).reshape(context, KVH, HD)
        row_values = jnp.take(pool_values, blocks, axis=0).reshape(context, KVH, HD)
        row_keys = jnp.concatenate([row_keys, new_keys.reshape(STEPS, KVH, HD)], axis=0).astype(jnp.float32)
        row_values = jnp.concatenate([row_values, new_values.reshape(STEPS, KVH, HD)], axis=0).astype(jnp.float32)
        allowed = jnp.where(seen_index[None, :] < context, seen_index[None, :] < length, seen_index[None, :] - context <= step_index[:, None])
        shaped = row_queries.reshape(STEPS, KVH, group_size, HD).astype(jnp.float32)
        attended = soft_attend(shaped, row_keys, row_values, allowed[:, None, None, :], score_scale, 'sgqd,kgd->sgqk', 'sgqk,kgd->sgqd')
        return attended.reshape(STEPS, D)
    decoded = lax.map(per_row, (row_blocks, context_lens, decode_queries.transpose(1, 0, 2), decode_keys.transpose(1, 0, 2), decode_values.transpose(1, 0, 2)))
    decode_attended = decoded.transpose(1, 0, 2)
    return (span_attended, decode_attended, span_cache)
```

```python
import functools
import math

import jax
import jax.numpy as jnp
import numpy as np
from jax import lax
from jax.experimental import pallas as pl
from jax.experimental.pallas import tpu as pltpu
from jax.sharding import PartitionSpec as P

D = 8192
H = 64
KVH = 8
HD = 128
PAGE = 16
STEPS = 2
BLK_ROW = 32


epsilon = 1e-05
neg_fill = -1e30
rotation_bits = 20


def normalize(row_block, gain_vector):
    widened = row_block.astype(jnp.float32)
    mean_square = jnp.mean(widened * widened, axis=-1, keepdims=True)
    return (widened * lax.rsqrt(mean_square + epsilon) * gain_vector.astype(jnp.float32)).astype(
        jnp.bfloat16
    )


def llama_frequencies(half_width):
    exponents = np.arange(half_width) / (1.0 * half_width)
    inverse = 1.0 / 500000.0**exponents
    wavelen = 2.0 * np.pi / inverse
    scaled = np.where(wavelen > 8192.0, inverse / 8.0, inverse)
    smooth = (8192.0 / wavelen - 1.0) / 3.0
    blended = (1.0 - smooth) * inverse / 8.0 + smooth * inverse
    middle = (wavelen >= 2048.0) & (wavelen <= 8192.0)
    return np.where(middle, blended, scaled)


def rotation_tables(half_width):
    frequencies = llama_frequencies(half_width)
    powers = 2.0 ** np.arange(rotation_bits)
    angles = powers[:, None] * frequencies[None, :]
    return (jnp.asarray(np.cos(angles), jnp.float32), jnp.asarray(np.sin(angles), jnp.float32))


VMEM_BYTES = 60 * 1024 * 1024
VMEM_SPEC = pl.BlockSpec(memory_space=pltpu.VMEM)


def greet(count, me):
    barrier = pltpu.get_barrier_semaphore()

    def signal(i, carry):
        pl.semaphore_signal(
            barrier,
            inc=1,
            device_id={"tensor": lax.rem(me + i, count)},
            device_id_type=pl.DeviceIdType.MESH,
        )
        return carry

    lax.fori_loop(1, count, signal, 0)
    pl.semaphore_wait(barrier, count - 1)


def spread_kernel(count, arrays, *refs):
    sources, targets = refs[:arrays], refs[arrays : 2 * arrays]
    send_sems, recv_sems, local_sems = refs[2 * arrays :]
    me = lax.axis_index("tensor")
    locals_ = [
        pltpu.make_async_copy(sources[a], targets[a].at[me], local_sems.at[a])
        for a in range(arrays)
    ]
    for copy in locals_:
        copy.start()
    greet(count, me)

    def remote(a, i):
        return pltpu.make_async_remote_copy(
            src_ref=sources[a],
            dst_ref=targets[a].at[me],
            send_sem=send_sems.at[a, i],
            recv_sem=recv_sems.at[a, i],
            device_id={"tensor": lax.rem(me + i, count)},
            device_id_type=pl.DeviceIdType.MESH,
        )

    def start(i, carry):
        for a in range(arrays):
            remote(a, i).start()
        return carry

    def finish(i, carry):
        for a in range(arrays):
            remote(a, i).wait()
        return carry

    lax.fori_loop(1, count, start, 0)
    for copy in locals_:
        copy.wait()
    lax.fori_loop(1, count, finish, 0)


def spread(parts, count, collective_id):
    arrays = len(parts)
    return pl.pallas_call(
        functools.partial(spread_kernel, count, arrays),
        out_shape=[jax.ShapeDtypeStruct((count,) + p.shape, p.dtype) for p in parts],
        in_specs=[VMEM_SPEC] * arrays,
        out_specs=[VMEM_SPEC] * arrays,
        scratch_shapes=[
            pltpu.SemaphoreType.DMA((arrays, count)),
            pltpu.SemaphoreType.DMA((arrays, count)),
            pltpu.SemaphoreType.DMA((arrays,)),
        ],
        compiler_params=pltpu.CompilerParams(
            collective_id=collective_id, has_side_effects=True, vmem_limit_bytes=VMEM_BYTES
        ),
        name=f"spread_{collective_id}",
    )(*parts)


def attend_kernel(
    count,
    heads_at_once,
    q_ref,
    kv_ref,
    pk_ref,
    pv_ref,
    dk_ref,
    dv_ref,
    map_ref,
    pos_ref,
    cos_ref,
    sin_ref,
    part_ref,
    stat_ref,
    cache_ref,
    turn_cos,
    turn_sin,
    wide,
    stats,
):
    me = lax.axis_index("tensor")
    f32 = jnp.float32
    bf16 = jnp.bfloat16
    total = pos_ref.shape[0]
    group = H // KVH
    scale = 1.0 / math.sqrt(HD)
    positions = pos_ref[...]
    cos_part = jnp.ones((total, HD), f32)
    sin_part = jnp.zeros((total, HD), f32)
    for bit in range(rotation_bits):
        chosen = (positions >> bit & 1).astype(f32)
        step_cos = 1.0 + chosen * (cos_ref[bit : bit + 1, :] - 1.0)
        step_sin = chosen * sin_ref[bit : bit + 1, :]
        cos_part, sin_part = (
            cos_part * step_cos - sin_part * step_sin,
            sin_part * step_cos + cos_part * step_sin,
        )
    lanes = lax.broadcasted_iota(jnp.int32, (total, HD), 1)
    turn_cos[...] = cos_part
    turn_sin[...] = jnp.where(lanes < HD // 2, -sin_part, sin_part)

    def turn(x):
        wide_x = x.astype(f32)
        return (wide_x * turn_cos[...] + pltpu.roll(wide_x, HD // 2, 1) * turn_sin[...]).astype(bf16)

    prefix_dev = pk_ref.shape[0]
    slot = lax.broadcasted_iota(jnp.int32, (1, prefix_dev), 1)
    prefix_seen = me * prefix_dev + slot < positions[0:1, :]

    pool_dev = dk_ref.shape[0]
    block_dev = pool_dev // PAGE
    token = lax.broadcasted_iota(jnp.int32, (1, pool_dev), 1)
    block_of = me * block_dev + token // PAGE
    entries = map_ref.shape[0]
    entry = lax.broadcasted_iota(jnp.int32, (entries, 1), 0)
    found = jnp.sum(jnp.where(map_ref[...] == block_of, entry, 0), axis=0, keepdims=True)
    row_of = found // BLK_ROW
    place = (found % BLK_ROW) * PAGE + token % PAGE
    row_ids = lax.broadcasted_iota(jnp.int32, (count, 1), 0)
    lens = positions[count : 2 * count, :]
    length = jnp.sum(jnp.where(row_ids == row_of, lens, 0), axis=0, keepdims=True)
    key_row = jnp.where(place < length, row_of, -1)

    nh = heads_at_once
    span_q = lax.broadcasted_iota(jnp.int32, (nh * count, 1), 0) % count
    own_j = lax.broadcasted_iota(jnp.int32, (1, count), 1)
    span_own = (own_j == me) & (own_j <= span_q)
    dec_q = lax.broadcasted_iota(jnp.int32, (nh * STEPS * count, 1), 0)
    dec_row = dec_q % count
    dec_step = (dec_q // count) % STEPS
    new_j = lax.broadcasted_iota(jnp.int32, (1, STEPS * count), 1)
    dec_own = (new_j % count == me) & (dec_row == me) & (new_j // count <= dec_step)
    pick = lax.broadcasted_iota(jnp.int32, (count, 1), 0) == me
    stat_lane = lax.broadcasted_iota(jnp.int32, (count, 2 * H), 1)
    stats[...] = jnp.zeros_like(stats)
    stat_ref[...] = jnp.zeros_like(stat_ref)
    across = (((1,), (1,)), ((), ()))

    def soft(q, keys, values, seen, keys2, values2, seen2):
        s1 = lax.dot_general(q, keys, across, preferred_element_type=f32) * scale
        s2 = lax.dot_general(q, keys2, across, preferred_element_type=f32) * scale
        s1 = jnp.where(seen, s1, neg_fill)
        s2 = jnp.where(seen2, s2, neg_fill)
        top = jnp.maximum(
            jnp.max(s1, axis=1, keepdims=True), jnp.max(s2, axis=1, keepdims=True)
        )
        w1 = jnp.where(seen, jnp.exp(s1 - top), 0.0)
        w2 = jnp.where(seen2, jnp.exp(s2 - top), 0.0)
        den = jnp.sum(w1, axis=1, keepdims=True) + jnp.sum(w2, axis=1, keepdims=True)
        num = jnp.dot(w1.astype(bf16), values, preferred_element_type=f32) + jnp.dot(
            w2.astype(bf16), values2, preferred_element_type=f32
        )
        return top, den, num

    def per_head(g, carry):
        cols = pl.ds(pl.multiple_of(g * HD, HD), HD)
        new_keys = turn(kv_ref[g])
        new_values = kv_ref[KVH + g]
        cache_ref[pl.ds(g, 1), :] = jnp.sum(
            jnp.where(pick, new_keys[:count].astype(f32), 0.0), axis=0, keepdims=True
        )
        cache_ref[pl.ds(KVH + g, 1), :] = jnp.sum(
            jnp.where(pick, new_values[:count].astype(f32), 0.0), axis=0, keepdims=True
        )
        for first in range(0, group, nh):
            turned = [turn(q_ref[g * group + first + i]) for i in range(nh)]
            span_queries = jnp.concatenate([t[:count] for t in turned], axis=0)
            dec_queries = jnp.concatenate([t[count:] for t in turned], axis=0)
            span_top, span_den, span_num = soft(
                span_queries,
                pk_ref[:, cols],
                pv_ref[:, cols],
                prefix_seen,
                new_keys[:count],
                new_values[:count],
                span_own,
            )
            dec_top, dec_den, dec_num = soft(
                dec_queries,
                dk_ref[:, cols],
                dv_ref[:, cols],
                key_row == dec_row,
                new_keys[count:],
                new_values[count:],
                dec_own,
            )
            for i in range(nh):
                head = g * group + first + i
                for kind in range(1 + STEPS):
                    if kind == 0:
                        rows = slice(i * count, (i + 1) * count)
                        top, den, num = span_top[rows], span_den[rows], span_num[rows]
                    else:
                        at = (i * STEPS + kind - 1) * count
                        rows = slice(at, at + count)
                        top, den, num = dec_top[rows], dec_den[rows], dec_num[rows]
                    wide[kind, pl.ds(head, count, stride=H), :] = num
                    stats[kind] = jnp.where(
                        stat_lane == head,
                        top,
                        jnp.where(stat_lane == H + head, den, stats[kind]),
                    )
        return carry

    lax.fori_loop(0, KVH, per_head, 0)
    for kind in range(1 + STEPS):
        stat_ref[pl.ds(kind, count, stride=8), :] = stats[kind]

    def pack(d, carry):
        for kind in range(1 + STEPS):
            rows = pl.ds(pl.multiple_of(d * H, H), H)
            part_ref[d, kind * H : (kind + 1) * H, :] = wide[kind, rows, :].astype(bf16)
        return carry

    lax.fori_loop(0, count, pack, 0)


def merge_kernel(count, part_ref, stat_ref, out_ref, parts, stats, send_sems, recv_sems, local_sems):
    me = lax.axis_index("tensor")
    f32 = jnp.float32
    sources, targets = (part_ref, stat_ref), (parts, stats)
    locals_ = [
        pltpu.make_async_copy(sources[a].at[me], targets[a].at[me], local_sems.at[a])
        for a in range(2)
    ]
    for copy in locals_:
        copy.start()
    greet(count, me)

    def remote(a, i):
        peer = lax.rem(me + i, count)
        return pltpu.make_async_remote_copy(
            src_ref=sources[a].at[peer],
            dst_ref=targets[a].at[me],
            send_sem=send_sems.at[a, i],
            recv_sem=recv_sems.at[a, i],
            device_id={"tensor": peer},
            device_id_type=pl.DeviceIdType.MESH,
        )

    def start(i, carry):
        for a in range(2):
            remote(a, i).start()
        return carry

    def finish(i, carry):
        for a in range(2):
            remote(a, i).wait()
        return carry

    lax.fori_loop(1, count, start, 0)
    for copy in locals_:
        copy.wait()
    lax.fori_loop(1, count, finish, 0)
    top = stats[0]
    for d in range(1, count):
        top = jnp.maximum(top, stats[d])
    den = jnp.zeros_like(top)
    for d in range(count):
        den = den + jnp.exp(stats[d] - top) * pltpu.roll(stats[d], H, 1)
    inverse = 1.0 / den
    share = jnp.concatenate([jnp.exp(stats[d] - top) * inverse for d in range(count)], axis=0).T
    for kind in range(1 + STEPS):
        acc = jnp.zeros((H, HD), f32)
        for d in range(count):
            acc = acc + share[:H, d * 8 + kind : d * 8 + kind + 1] * parts[
                d, kind * H : (kind + 1) * H, :
            ].astype(f32)
        out_ref[kind] = acc.astype(out_ref.dtype)


def shards(
    span_rows,
    decode_rows,
    norm_gain,
    w_query,
    w_keyval,
    prefix_keys,
    prefix_values,
    span_offset,
    pool_keys,
    pool_values,
    row_blocks,
    context_lens,
):
    count = lax.axis_size("tensor")
    span_dev = span_rows.shape[0]
    rows_dev = decode_rows.shape[1]
    assert span_dev == 1 and rows_dev == 1
    kinds = 1 + STEPS
    local_rows = jnp.concatenate([span_rows, decode_rows.reshape(STEPS, D)], axis=0)
    normed = normalize(local_rows, norm_gain)
    (gathered,) = spread([normed.reshape(kinds * 16, D // 16)], count, 0)
    shard_rows = gathered.reshape(count, kinds, D).transpose(1, 0, 2).reshape(kinds * count, D)
    total = kinds * count
    queries = jnp.dot(shard_rows, w_query, preferred_element_type=jnp.float32).astype(jnp.bfloat16)
    keyval = jnp.dot(shard_rows, w_keyval, preferred_element_type=jnp.float32).astype(jnp.bfloat16)

    def split(x):
        if x.shape[1] % HD == 0:
            return x.reshape(total, -1, HD).transpose(1, 0, 2)
        return x

    def join(x):
        if x.ndim == 4:
            return x.reshape(-1, total, HD)
        return x.transpose(1, 0, 2).reshape(total, -1, HD).transpose(1, 0, 2)

    all_q, all_kv = spread([split(queries), split(keyval)], count, 1)
    q_heads, kv_heads = join(all_q), join(all_kv)
    offset = span_offset[0]
    positions = jnp.concatenate(
        [offset + jnp.arange(count, dtype=jnp.int32)] + [context_lens + s for s in range(STEPS)]
    )[:, None]
    cos_table, sin_table = rotation_tables(HD // 2)
    tile = lambda x: jnp.concatenate([x, x], axis=1)
    part, stat, cache = pl.pallas_call(
        functools.partial(attend_kernel, count, H // KVH if count <= 32 else 1),
        out_shape=[
            jax.ShapeDtypeStruct((count, kinds * H, HD), jnp.bfloat16),
            jax.ShapeDtypeStruct((count * 8, 2 * H), jnp.float32),
            jax.ShapeDtypeStruct((2 * KVH, HD), jnp.float32),
        ],
        in_specs=[VMEM_SPEC] * 10,
        out_specs=[VMEM_SPEC] * 3,
        scratch_shapes=[
            pltpu.VMEM((total, HD), jnp.float32),
            pltpu.VMEM((total, HD), jnp.float32),
            pltpu.VMEM((kinds, count * H, HD), jnp.float32),
            pltpu.VMEM((kinds, count, 2 * H), jnp.float32),
        ],
        compiler_params=pltpu.CompilerParams(vmem_limit_bytes=VMEM_BYTES),
        name="attend",
    )(
        q_heads,
        kv_heads,
        prefix_keys,
        prefix_values,
        pool_keys.reshape(-1, KVH * HD),
        pool_values.reshape(-1, KVH * HD),
        row_blocks.reshape(-1, 1),
        positions,
        tile(cos_table),
        tile(sin_table),
    )
    merged = pl.pallas_call(
        functools.partial(merge_kernel, count),
        out_shape=jax.ShapeDtypeStruct((kinds, H, HD), jnp.bfloat16),
        in_specs=[VMEM_SPEC] * 2,
        out_specs=VMEM_SPEC,
        scratch_shapes=[
            pltpu.VMEM((count, kinds * H, HD), jnp.bfloat16),
            pltpu.VMEM((count, 8, 2 * H), jnp.float32),
            pltpu.SemaphoreType.DMA((2, count)),
            pltpu.SemaphoreType.DMA((2, count)),
            pltpu.SemaphoreType.DMA((2,)),
        ],
        compiler_params=pltpu.CompilerParams(
            collective_id=2, has_side_effects=True, vmem_limit_bytes=VMEM_BYTES
        ),
        name="merge",
    )(part, stat.reshape(count, 8, 2 * H))
    span_attended = merged[0].reshape(1, D)
    decode_attended = merged[1:].reshape(STEPS, 1, D)
    span_cache = cache.reshape(1, 2 * KVH * HD).astype(jnp.bfloat16)
    return (span_attended, decode_attended, span_cache)


def solution(mesh):
    in_specs = (
        P(("groups", "tensor"), None),
        P(None, ("groups", "tensor"), None),
        P(),
        P(None, "tensor"),
        P(None, "tensor"),
        P(("groups", "tensor"), None),
        P(("groups", "tensor"), None),
        P("groups"),
        P(("groups", "tensor"), None, None),
        P(("groups", "tensor"), None, None),
        P("groups", None),
        P("groups"),
    )
    out_specs = (
        P(("groups", "tensor"), None),
        P(None, ("groups", "tensor"), None),
        P(("groups", "tensor"), None),
    )
    return jax.shard_map(shards, mesh=mesh, in_specs=in_specs, out_specs=out_specs, check_vma=False)
```

```python
import functools
import math

import jax
import jax.numpy as jnp
import numpy as np
from jax import lax
from jax.experimental import pallas as pl
from jax.experimental.pallas import tpu as pltpu
from jax.sharding import PartitionSpec as P

D = 8192
H = 64
KVH = 8
HD = 128
PAGE = 16
STEPS = 2
BLK_ROW = 32


epsilon = 1e-05
neg_fill = -1e30
rotation_bits = 20


def normalize(row_block, gain_vector):
    widened = row_block.astype(jnp.float32)
    mean_square = jnp.mean(widened * widened, axis=-1, keepdims=True)
    return (widened * lax.rsqrt(mean_square + epsilon) * gain_vector.astype(jnp.float32)).astype(
        jnp.bfloat16
    )


def llama_frequencies(half_width):
    exponents = np.arange(half_width) / (1.0 * half_width)
    inverse = 1.0 / 500000.0**exponents
    wavelen = 2.0 * np.pi / inverse
    scaled = np.where(wavelen > 8192.0, inverse / 8.0, inverse)
    smooth = (8192.0 / wavelen - 1.0) / 3.0
    blended = (1.0 - smooth) * inverse / 8.0 + smooth * inverse
    middle = (wavelen >= 2048.0) & (wavelen <= 8192.0)
    return np.where(middle, blended, scaled)


def rotation_tables(half_width):
    frequencies = llama_frequencies(half_width)
    powers = 2.0 ** np.arange(rotation_bits)
    angles = powers[:, None] * frequencies[None, :]
    return (jnp.asarray(np.cos(angles), jnp.float32), jnp.asarray(np.sin(angles), jnp.float32))


VMEM_BYTES = 60 * 1024 * 1024
VMEM_SPEC = pl.BlockSpec(memory_space=pltpu.VMEM)


def greet(count, me):
    barrier = pltpu.get_barrier_semaphore()

    def signal(i, carry):
        pl.semaphore_signal(
            barrier,
            inc=1,
            device_id={"tensor": lax.rem(me + i, count)},
            device_id_type=pl.DeviceIdType.MESH,
        )
        return carry

    lax.fori_loop(1, count, signal, 0)
    pl.semaphore_wait(barrier, count - 1)


def layout_of(mesh):
    count = mesh.shape["tensor"]
    line = mesh.devices.reshape(-1, count)[0]
    coords = [tuple(getattr(device, "coords", (i,))) for i, device in enumerate(line)]
    cores = sum(1 for c in coords if c == coords[0])
    chips = coords[::cores]
    inner = 1
    if len(chips) > 1:
        axis = [p != q for p, q in zip(chips[0], chips[1])].index(True)
        inner = len({c[axis] for c in chips})
    if count % (cores * inner):
        return count, 1, 1
    return count // (cores * inner), inner, cores


def spread_copies(layout, source, target, send_sems, recv_sems):
    outer, inner, cores = layout
    me = lax.axis_index("tensor")
    core = lax.rem(me, cores)
    column = lax.rem(me // cores, inner)
    plane = me // (cores * inner)
    pending = []

    def index(z, y, c):
        return (z * inner + y) * cores + c

    def send(owner, src, peer, slot):
        copy = pltpu.make_async_remote_copy(
            src_ref=src,
            dst_ref=target.at[owner],
            send_sem=send_sems.at[slot],
            recv_sem=recv_sems.at[owner],
            device_id={"tensor": peer},
            device_id_type=pl.DeviceIdType.MESH,
        )
        copy.start()
        pending.append(copy)

    def arrived(owner):
        pltpu.make_async_remote_copy(
            src_ref=source,
            dst_ref=target.at[owner],
            send_sem=send_sems.at[0],
            recv_sem=recv_sems.at[owner],
            device_id={"tensor": index(plane, column, lax.rem(core + 1, cores))},
            device_id_type=pl.DeviceIdType.MESH,
        ).wait_recv()

    slots = iter(range(outer * inner * cores))
    for i in range(1, outer):
        send(me, source, index(lax.rem(plane + i, outer), column, core), next(slots))
    for j in range(outer):
        owner = index(lax.rem(plane + outer - j, outer), column, core)
        if j > 0:
            arrived(owner)
        src = source if j == 0 else target.at[owner]
        for k in range(1, inner):
            send(owner, src, index(plane, lax.rem(column + k, inner), core), next(slots))
        for k in range(1, cores):
            send(owner, src, index(plane, column, lax.rem(core + k, cores)), next(slots))
    for j in range(outer):
        for k in range(1, inner):
            owner = index(
                lax.rem(plane + outer - j, outer), lax.rem(column + inner - k, inner), core
            )
            arrived(owner)
            for n in range(1, cores):
                peer = index(plane, column, lax.rem(core + n, cores))
                send(owner, target.at[owner], peer, next(slots))
    for j in range(outer):
        for k in range(inner):
            for n in range(1, cores):
                arrived(
                    index(
                        lax.rem(plane + outer - j, outer),
                        lax.rem(column + inner - k, inner),
                        lax.rem(core + cores - n, cores),
                    )
                )
    for copy in pending:
        copy.wait_send()


def spread_kernel(layout, source, target, send_sems, recv_sems, local_sem):
    count = math.prod(layout)
    me = lax.axis_index("tensor")
    own = pltpu.make_async_copy(source, target.at[me], local_sem)
    own.start()
    greet(count, me)
    spread_copies(layout, source, target, send_sems, recv_sems)
    own.wait()


def spread(part, layout, collective_id):
    count = math.prod(layout)
    return pl.pallas_call(
        functools.partial(spread_kernel, layout),
        out_shape=jax.ShapeDtypeStruct((count,) + part.shape, part.dtype),
        in_specs=[VMEM_SPEC],
        out_specs=VMEM_SPEC,
        scratch_shapes=[
            pltpu.SemaphoreType.DMA((count,)),
            pltpu.SemaphoreType.DMA((count,)),
            pltpu.SemaphoreType.DMA,
        ],
        compiler_params=pltpu.CompilerParams(
            collective_id=collective_id, has_side_effects=True, vmem_limit_bytes=VMEM_BYTES
        ),
        name=f"spread_{collective_id}",
    )(part)


def attend_kernel(
    count,
    heads_at_once,
    per_dev,
    all_ref,
    pk_ref,
    pv_ref,
    dk_ref,
    dv_ref,
    map_ref,
    pos_ref,
    cos_ref,
    sin_ref,
    part_ref,
    stat_ref,
    cache_ref,
    turn_cos,
    turn_sin,
    wide,
    stats,
):
    me = lax.axis_index("tensor")
    f32 = jnp.float32
    bf16 = jnp.bfloat16
    total = pos_ref.shape[0]
    group = H // KVH
    q_dev, kv_dev = per_dev

    def q_head(h):
        return all_ref[h // q_dev, h % q_dev]

    def kv_head(j):
        return all_ref[j // kv_dev, q_dev + j % kv_dev]

    scale = 1.0 / math.sqrt(HD)
    positions = pos_ref[...]
    cos_part = jnp.ones((total, HD), f32)
    sin_part = jnp.zeros((total, HD), f32)
    for bit in range(rotation_bits):
        chosen = (positions >> bit & 1).astype(f32)
        step_cos = 1.0 + chosen * (cos_ref[bit : bit + 1, :] - 1.0)
        step_sin = chosen * sin_ref[bit : bit + 1, :]
        cos_part, sin_part = (
            cos_part * step_cos - sin_part * step_sin,
            sin_part * step_cos + cos_part * step_sin,
        )
    lanes = lax.broadcasted_iota(jnp.int32, (total, HD), 1)
    turn_cos[...] = cos_part
    turn_sin[...] = jnp.where(lanes < HD // 2, -sin_part, sin_part)

    def turn(x):
        wide_x = x.astype(f32)
        return (wide_x * turn_cos[...] + pltpu.roll(wide_x, HD // 2, 1) * turn_sin[...]).astype(bf16)

    prefix_dev = pk_ref.shape[0]
    slot = lax.broadcasted_iota(jnp.int32, (1, prefix_dev), 1)
    prefix_seen = me * prefix_dev + slot < positions[0:1, :]

    pool_dev = dk_ref.shape[0]
    block_dev = pool_dev // PAGE
    token = lax.broadcasted_iota(jnp.int32, (1, pool_dev), 1)
    block_of = me * block_dev + token // PAGE
    entries = map_ref.shape[0]
    entry = lax.broadcasted_iota(jnp.int32, (entries, 1), 0)
    found = jnp.sum(jnp.where(map_ref[...] == block_of, entry, 0), axis=0, keepdims=True)
    row_of = found // BLK_ROW
    place = (found % BLK_ROW) * PAGE + token % PAGE
    row_ids = lax.broadcasted_iota(jnp.int32, (count, 1), 0)
    lens = positions[count : 2 * count, :]
    length = jnp.sum(jnp.where(row_ids == row_of, lens, 0), axis=0, keepdims=True)
    key_row = jnp.where(place < length, row_of, -1)

    nh = heads_at_once
    span_q = lax.broadcasted_iota(jnp.int32, (nh * count, 1), 0) % count
    own_j = lax.broadcasted_iota(jnp.int32, (1, count), 1)
    span_own = (own_j == me) & (own_j <= span_q)
    dec_q = lax.broadcasted_iota(jnp.int32, (nh * STEPS * count, 1), 0)
    dec_row = dec_q % count
    dec_step = (dec_q // count) % STEPS
    new_j = lax.broadcasted_iota(jnp.int32, (1, STEPS * count), 1)
    dec_own = (new_j % count == me) & (dec_row == me) & (new_j // count <= dec_step)
    pick = lax.broadcasted_iota(jnp.int32, (count, 1), 0) == me
    stat_lane = lax.broadcasted_iota(jnp.int32, (count, 2 * H), 1)
    stats[...] = jnp.zeros_like(stats)
    stat_ref[...] = jnp.zeros_like(stat_ref)
    across = (((1,), (1,)), ((), ()))

    def soft(q, keys, values, seen, keys2, values2, seen2):
        s1 = lax.dot_general(q, keys, across, preferred_element_type=f32) * scale
        s2 = lax.dot_general(q, keys2, across, preferred_element_type=f32) * scale
        s1 = jnp.where(seen, s1, neg_fill)
        s2 = jnp.where(seen2, s2, neg_fill)
        top = jnp.maximum(
            jnp.max(s1, axis=1, keepdims=True), jnp.max(s2, axis=1, keepdims=True)
        )
        w1 = jnp.where(seen, jnp.exp(s1 - top), 0.0)
        w2 = jnp.where(seen2, jnp.exp(s2 - top), 0.0)
        den = jnp.sum(w1, axis=1, keepdims=True) + jnp.sum(w2, axis=1, keepdims=True)
        num = jnp.dot(w1.astype(bf16), values, preferred_element_type=f32) + jnp.dot(
            w2.astype(bf16), values2, preferred_element_type=f32
        )
        return top, den, num

    def per_head(g, carry):
        cols = pl.ds(pl.multiple_of(g * HD, HD), HD)
        new_keys = turn(kv_head(g))
        new_values = kv_head(KVH + g)
        cache_ref[pl.ds(g, 1), :] = jnp.sum(
            jnp.where(pick, new_keys[:count].astype(f32), 0.0), axis=0, keepdims=True
        )
        cache_ref[pl.ds(KVH + g, 1), :] = jnp.sum(
            jnp.where(pick, new_values[:count].astype(f32), 0.0), axis=0, keepdims=True
        )
        for first in range(0, group, nh):
            turned = [turn(q_head(g * group + first + i)) for i in range(nh)]
            span_queries = jnp.concatenate([t[:count] for t in turned], axis=0)
            dec_queries = jnp.concatenate([t[count:] for t in turned], axis=0)
            span_top, span_den, span_num = soft(
                span_queries,
                pk_ref[:, cols],
                pv_ref[:, cols],
                prefix_seen,
                new_keys[:count],
                new_values[:count],
                span_own,
            )
            dec_top, dec_den, dec_num = soft(
                dec_queries,
                dk_ref[:, cols],
                dv_ref[:, cols],
                key_row == dec_row,
                new_keys[count:],
                new_values[count:],
                dec_own,
            )
            for i in range(nh):
                head = g * group + first + i
                for kind in range(1 + STEPS):
                    if kind == 0:
                        rows = slice(i * count, (i + 1) * count)
                        top, den, num = span_top[rows], span_den[rows], span_num[rows]
                    else:
                        at = (i * STEPS + kind - 1) * count
                        rows = slice(at, at + count)
                        top, den, num = dec_top[rows], dec_den[rows], dec_num[rows]
                    wide[kind, pl.ds(head, count, stride=H), :] = num
                    stats[kind] = jnp.where(
                        stat_lane == head,
                        top,
                        jnp.where(stat_lane == H + head, den, stats[kind]),
                    )
        return carry

    lax.fori_loop(0, KVH, per_head, 0)
    for kind in range(1 + STEPS):
        stat_ref[pl.ds(kind, count, stride=8), :] = stats[kind]

    def pack(d, carry):
        for kind in range(1 + STEPS):
            rows = pl.ds(pl.multiple_of(d * H, H), H)
            part_ref[d, kind * H : (kind + 1) * H, :] = wide[kind, rows, :].astype(bf16)
        return carry

    lax.fori_loop(0, count, pack, 0)


def merge_kernel(count, part_ref, stat_ref, out_ref, parts, stats, send_sems, recv_sems, local_sems):
    me = lax.axis_index("tensor")
    f32 = jnp.float32
    sources, targets = (part_ref, stat_ref), (parts, stats)
    locals_ = [
        pltpu.make_async_copy(sources[a].at[me], targets[a].at[me], local_sems.at[a])
        for a in range(2)
    ]
    for copy in locals_:
        copy.start()
    greet(count, me)

    def remote(a, i):
        peer = lax.rem(me + i, count)
        return pltpu.make_async_remote_copy(
            src_ref=sources[a].at[peer],
            dst_ref=targets[a].at[me],
            send_sem=send_sems.at[a, i],
            recv_sem=recv_sems.at[a, i],
            device_id={"tensor": peer},
            device_id_type=pl.DeviceIdType.MESH,
        )

    def start(i, carry):
        for a in range(2):
            remote(a, i).start()
        return carry

    def finish(i, carry):
        for a in range(2):
            remote(a, i).wait()
        return carry

    lax.fori_loop(1, count, start, 0)
    for copy in locals_:
        copy.wait()
    lax.fori_loop(1, count, finish, 0)
    top = stats[0]
    for d in range(1, count):
        top = jnp.maximum(top, stats[d])
    den = jnp.zeros_like(top)
    for d in range(count):
        den = den + jnp.exp(stats[d] - top) * pltpu.roll(stats[d], H, 1)
    inverse = 1.0 / den
    share = jnp.concatenate([jnp.exp(stats[d] - top) * inverse for d in range(count)], axis=0).T
    for kind in range(1 + STEPS):
        acc = jnp.zeros((H, HD), f32)
        for d in range(count):
            acc = acc + share[:H, d * 8 + kind : d * 8 + kind + 1] * parts[
                d, kind * H : (kind + 1) * H, :
            ].astype(f32)
        out_ref[kind] = acc.astype(out_ref.dtype)


def shards(
    layout,
    span_rows,
    decode_rows,
    norm_gain,
    w_query,
    w_keyval,
    prefix_keys,
    prefix_values,
    span_offset,
    pool_keys,
    pool_values,
    row_blocks,
    context_lens,
):
    count = lax.axis_size("tensor")
    span_dev = span_rows.shape[0]
    rows_dev = decode_rows.shape[1]
    assert span_dev == 1 and rows_dev == 1
    kinds = 1 + STEPS
    local_rows = jnp.concatenate([span_rows, decode_rows.reshape(STEPS, D)], axis=0)
    normed = normalize(local_rows, norm_gain)
    gathered = spread(normed.reshape(kinds * 16, D // 16), layout, 0)
    shard_rows = gathered.reshape(count, kinds, D).transpose(1, 0, 2).reshape(kinds * count, D)
    total = kinds * count
    queries = jnp.dot(shard_rows, w_query, preferred_element_type=jnp.float32).astype(jnp.bfloat16)
    keyval = jnp.dot(shard_rows, w_keyval, preferred_element_type=jnp.float32).astype(jnp.bfloat16)

    q_dev, kv_dev = queries.shape[1] // HD, keyval.shape[1] // HD
    if queries.shape[1] % HD == 0 and keyval.shape[1] % HD == 0:
        heads = jnp.concatenate([queries, keyval], axis=1).reshape(total, -1, HD)
        heads = spread(heads.transpose(1, 0, 2), layout, 1)
    else:
        cut = queries.shape[1]
        heads = spread(jnp.concatenate([queries, keyval], axis=1), layout, 1).transpose(1, 0, 2)
        heads = jnp.concatenate(
            [heads[:, :, :cut].reshape(total, -1, HD), heads[:, :, cut:].reshape(total, -1, HD)],
            axis=1,
        ).transpose(1, 0, 2)[None]
        q_dev, kv_dev = H, 2 * KVH
    offset = span_offset[0]
    positions = jnp.concatenate(
        [offset + jnp.arange(count, dtype=jnp.int32)] + [context_lens + s for s in range(STEPS)]
    )[:, None]
    cos_table, sin_table = rotation_tables(HD // 2)
    tile = lambda x: jnp.concatenate([x, x], axis=1)
    part, stat, cache = pl.pallas_call(
        functools.partial(
            attend_kernel, count, H // KVH if count <= 32 else 1, (q_dev, kv_dev)
        ),
        out_shape=[
            jax.ShapeDtypeStruct((count, kinds * H, HD), jnp.bfloat16),
            jax.ShapeDtypeStruct((count * 8, 2 * H), jnp.float32),
            jax.ShapeDtypeStruct((2 * KVH, HD), jnp.float32),
        ],
        in_specs=[VMEM_SPEC] * 9,
        out_specs=[VMEM_SPEC] * 3,
        scratch_shapes=[
            pltpu.VMEM((total, HD), jnp.float32),
            pltpu.VMEM((total, HD), jnp.float32),
            pltpu.VMEM((kinds, count * H, HD), jnp.float32),
            pltpu.VMEM((kinds, count, 2 * H), jnp.float32),
        ],
        compiler_params=pltpu.CompilerParams(vmem_limit_bytes=VMEM_BYTES),
        name="attend",
    )(
        heads,
        prefix_keys,
        prefix_values,
        pool_keys.reshape(-1, KVH * HD),
        pool_values.reshape(-1, KVH * HD),
        row_blocks.reshape(-1, 1),
        positions,
        tile(cos_table),
        tile(sin_table),
    )
    merged = pl.pallas_call(
        functools.partial(merge_kernel, count),
        out_shape=jax.ShapeDtypeStruct((kinds, H, HD), jnp.bfloat16),
        in_specs=[VMEM_SPEC] * 2,
        out_specs=VMEM_SPEC,
        scratch_shapes=[
            pltpu.VMEM((count, kinds * H, HD), jnp.bfloat16),
            pltpu.VMEM((count, 8, 2 * H), jnp.float32),
            pltpu.SemaphoreType.DMA((2, count)),
            pltpu.SemaphoreType.DMA((2, count)),
            pltpu.SemaphoreType.DMA((2,)),
        ],
        compiler_params=pltpu.CompilerParams(
            collective_id=2, has_side_effects=True, vmem_limit_bytes=VMEM_BYTES
        ),
        name="merge",
    )(part, stat.reshape(count, 8, 2 * H))
    span_attended = merged[0].reshape(1, D)
    decode_attended = merged[1:].reshape(STEPS, 1, D)
    span_cache = cache.reshape(1, 2 * KVH * HD).astype(jnp.bfloat16)
    return (span_attended, decode_attended, span_cache)


def solution(mesh):
    in_specs = (
        P(("groups", "tensor"), None),
        P(None, ("groups", "tensor"), None),
        P(),
        P(None, "tensor"),
        P(None, "tensor"),
        P(("groups", "tensor"), None),
        P(("groups", "tensor"), None),
        P("groups"),
        P(("groups", "tensor"), None, None),
        P(("groups", "tensor"), None, None),
        P("groups", None),
        P("groups"),
    )
    out_specs = (
        P(("groups", "tensor"), None),
        P(None, ("groups", "tensor"), None),
        P(("groups", "tensor"), None),
    )
    return jax.shard_map(
        functools.partial(shards, layout_of(mesh)),
        mesh=mesh,
        in_specs=in_specs,
        out_specs=out_specs,
        check_vma=False,
    )
```

```python
import functools
import math

import jax
import jax.numpy as jnp
import numpy as np
from jax import lax
from jax.experimental import pallas as pl
from jax.experimental.pallas import tpu as pltpu
from jax.sharding import PartitionSpec as P

D = 8192
H = 64
KVH = 8
HD = 128
PAGE = 16
STEPS = 2
BLK_ROW = 32


epsilon = 1e-05
neg_fill = -1e30
top_floor = -1e20
rotation_bits = 20


def llama_frequencies(half_width):
    exponents = np.arange(half_width) / (1.0 * half_width)
    inverse = 1.0 / 500000.0**exponents
    wavelen = 2.0 * np.pi / inverse
    scaled = np.where(wavelen > 8192.0, inverse / 8.0, inverse)
    smooth = (8192.0 / wavelen - 1.0) / 3.0
    blended = (1.0 - smooth) * inverse / 8.0 + smooth * inverse
    middle = (wavelen >= 2048.0) & (wavelen <= 8192.0)
    return np.where(middle, blended, scaled)


def rotation_tables(half_width):
    frequencies = llama_frequencies(half_width)
    powers = 2.0 ** np.arange(rotation_bits)
    angles = powers[:, None] * frequencies[None, :]
    return (jnp.asarray(np.cos(angles), jnp.float32), jnp.asarray(np.sin(angles), jnp.float32))


VMEM_BYTES = 60 * 1024 * 1024
VMEM_SPEC = pl.BlockSpec(memory_space=pltpu.VMEM)


def greet_all(count, me):
    barrier = pltpu.get_barrier_semaphore()

    def signal(i, carry):
        pl.semaphore_signal(
            barrier,
            inc=1,
            device_id={"tensor": lax.rem(me + i, count)},
            device_id_type=pl.DeviceIdType.MESH,
        )
        return carry

    lax.fori_loop(1, count, signal, 0)
    pl.semaphore_wait(barrier, count - 1)


def greet_near(layout):
    outer, inner, cores = layout
    me = lax.axis_index("tensor")
    core = lax.rem(me, cores)
    column = lax.rem(me // cores, inner)
    plane = me // (cores * inner)
    peers = [(lax.rem(plane + i, outer) * inner + column) * cores + core for i in range(1, outer)]
    peers += [(plane * inner + lax.rem(column + i, inner)) * cores + core for i in range(1, inner)]
    peers += [(plane * inner + column) * cores + lax.rem(core + i, cores) for i in range(1, cores)]
    barrier = pltpu.get_barrier_semaphore()
    for peer in peers:
        pl.semaphore_signal(
            barrier,
            inc=1,
            device_id={"tensor": peer},
            device_id_type=pl.DeviceIdType.MESH,
        )
    pl.semaphore_wait(barrier, len(peers))


def layout_of(mesh):
    count = mesh.shape["tensor"]
    line = mesh.devices.reshape(-1, count)[0]
    coords = [tuple(getattr(device, "coords", (i,))) for i, device in enumerate(line)]
    cores = sum(1 for c in coords if c == coords[0])
    chips = coords[::cores]
    inner = 1
    if len(chips) > 1:
        axis = [p != q for p, q in zip(chips[0], chips[1])].index(True)
        inner = len({c[axis] for c in chips})
    if count % (cores * inner):
        return count, 1, 1
    return count // (cores * inner), inner, cores


def spread_copies(layout, target, send_sems, recv_sems):
    outer, inner, cores = layout
    me = lax.axis_index("tensor")
    core = lax.rem(me, cores)
    column = lax.rem(me // cores, inner)
    plane = me // (cores * inner)
    pending = []
    source = target.at[me]

    def index(z, y, c):
        return (z * inner + y) * cores + c

    def send(owner, src, peer, slot):
        copy = pltpu.make_async_remote_copy(
            src_ref=src,
            dst_ref=target.at[owner],
            send_sem=send_sems.at[slot],
            recv_sem=recv_sems.at[owner],
            device_id={"tensor": peer},
            device_id_type=pl.DeviceIdType.MESH,
        )
        copy.start()
        pending.append(copy)

    def arrived(owner):
        pltpu.make_async_remote_copy(
            src_ref=source,
            dst_ref=target.at[owner],
            send_sem=send_sems.at[0],
            recv_sem=recv_sems.at[owner],
            device_id={"tensor": index(plane, column, lax.rem(core + 1, cores))},
            device_id_type=pl.DeviceIdType.MESH,
        ).wait_recv()

    slots = iter(range(outer * inner * cores))
    for i in range(1, outer):
        send(me, source, index(lax.rem(plane + i, outer), column, core), next(slots))
    for j in range(outer):
        owner = index(lax.rem(plane + outer - j, outer), column, core)
        if j > 0:
            arrived(owner)
        src = source if j == 0 else target.at[owner]
        for k in range(1, inner):
            send(owner, src, index(plane, lax.rem(column + k, inner), core), next(slots))
        for k in range(1, cores):
            send(owner, src, index(plane, column, lax.rem(core + k, cores)), next(slots))
    for j in range(outer):
        for k in range(1, inner):
            owner = index(
                lax.rem(plane + outer - j, outer), lax.rem(column + inner - k, inner), core
            )
            arrived(owner)
            for n in range(1, cores):
                peer = index(plane, column, lax.rem(core + n, cores))
                send(owner, target.at[owner], peer, next(slots))
    for j in range(outer):
        for k in range(inner):
            for n in range(1, cores):
                arrived(
                    index(
                        lax.rem(plane + outer - j, outer),
                        lax.rem(column + inner - k, inner),
                        lax.rem(core + cores - n, cores),
                    )
                )
    for copy in pending:
        copy.wait_send()


def front_kernel(
    layout,
    span_ref,
    decode_ref,
    gain_ref,
    wq_hbm,
    wkv_hbm,
    heads_ref,
    lines,
    gathered,
    spread_rows,
    wq_buf,
    wkv_buf,
    weight_sems,
    send_sems,
    recv_sems,
    send_sems2,
    recv_sems2,
):
    f32 = jnp.float32
    count = math.prod(layout)
    me = lax.axis_index("tensor")
    depth, pieces = wq_hbm.shape[0], weight_sems.shape[1]
    step = depth // pieces
    fetches = []
    for i in range(pieces):
        rows = pl.ds(i * step, step)
        for a, (src, dst) in enumerate(((wq_hbm, wq_buf), (wkv_hbm, wkv_buf))):
            copy = pltpu.make_async_copy(src.at[rows], dst.at[rows], weight_sems.at[a, i])
            copy.start()
            fetches.append(copy)
    gain = gain_ref[...].astype(f32)
    width = lines.shape[1]
    folds = depth // width
    kinds = lines.shape[0] // folds
    for first, ref in ((0, span_ref), (1, decode_ref)):
        x = ref[...].astype(f32)
        mean_square = jnp.mean(x * x, axis=-1, keepdims=True)
        x = x * lax.rsqrt(mean_square + epsilon) * gain
        for r in range(x.shape[0]):
            for k in range(folds):
                lines[pl.ds((first + r) * folds + k, 1), :] = x[
                    r : r + 1, k * width : (k + 1) * width
                ]
    gathered[me] = lines[...].astype(jnp.bfloat16)
    greet_near(layout)
    spread_copies(layout, gathered, send_sems, recv_sems)

    def widen(d, carry):
        rows = pl.ds(pl.multiple_of(d * kinds * folds, kinds * folds), kinds * folds)
        for j in range(width // HD):
            spread_rows[j, rows, :] = gathered[d, :, j * HD : (j + 1) * HD].astype(f32)
        return carry

    lax.fori_loop(0, count, widen, 0)
    total = kinds * count
    queries = jnp.zeros((total, wq_hbm.shape[1]), f32)
    keyval = jnp.zeros((total, wkv_hbm.shape[1]), f32)
    for k in range(folds):
        if k * width % step == 0:
            at = k * width // step
            fetches[2 * at].wait()
            fetches[2 * at + 1].wait()
        rows = jnp.concatenate(
            [
                jnp.concatenate(
                    [
                        spread_rows[j, pl.ds(kind * folds + k, count, stride=kinds * folds), :]
                        for kind in range(kinds)
                    ],
                    axis=0,
                )
                for j in range(width // HD)
            ],
            axis=1,
        ).astype(jnp.bfloat16)
        part = slice(k * width, (k + 1) * width)
        queries += jnp.dot(rows, wq_buf[part, :], preferred_element_type=f32)
        keyval += jnp.dot(rows, wkv_buf[part, :], preferred_element_type=f32)
    if len(heads_ref.shape) == 4:
        q_dev = queries.shape[1] // HD
        for h in range(heads_ref.shape[1]):
            x = queries if h < q_dev else keyval
            at = (h if h < q_dev else h - q_dev) * HD
            heads_ref[me, h] = x[:, at : at + HD].astype(jnp.bfloat16)
    else:
        heads_ref[me] = jnp.concatenate([queries, keyval], axis=1).astype(jnp.bfloat16)
    spread_copies(layout, heads_ref, send_sems2, recv_sems2)


def front(layout, span_rows, decode_rows, norm_gain, w_query, w_keyval):
    count = math.prod(layout)
    kinds = 1 + STEPS
    total = kinds * count
    depth, q_cols = w_query.shape
    kv_cols = w_keyval.shape[1]
    width = 512
    by_head = q_cols % HD == 0 and kv_cols % HD == 0
    heads = ((q_cols + kv_cols) // HD, total, HD) if by_head else (total, q_cols + kv_cols)
    dma = pltpu.SemaphoreType.DMA
    return pl.pallas_call(
        functools.partial(front_kernel, layout),
        out_shape=jax.ShapeDtypeStruct((count,) + heads, jnp.bfloat16),
        in_specs=[VMEM_SPEC] * 3 + [pl.BlockSpec(memory_space=pl.ANY)] * 2,
        out_specs=VMEM_SPEC,
        scratch_shapes=[
            pltpu.VMEM((kinds * depth // width, width), jnp.float32),
            pltpu.VMEM((count, kinds * depth // width, width), jnp.bfloat16),
            pltpu.VMEM((width // HD, count * kinds * depth // width, HD), jnp.float32),
            pltpu.VMEM(w_query.shape, jnp.bfloat16),
            pltpu.VMEM(w_keyval.shape, jnp.bfloat16),
            dma((2, 4)),
            dma((count,)),
            dma((count,)),
            dma((count,)),
            dma((count,)),
        ],
        compiler_params=pltpu.CompilerParams(
            collective_id=0, has_side_effects=True, vmem_limit_bytes=VMEM_BYTES
        ),
        name="front",
    )(span_rows, decode_rows.reshape(STEPS, depth), norm_gain.reshape(1, depth), w_query, w_keyval)


def attend_kernel(
    count,
    heads_at_once,
    per_dev,
    all_ref,
    pk_ref,
    pv_ref,
    dk_ref,
    dv_ref,
    map_ref,
    offset_ref,
    lens_ref,
    cos_ref,
    sin_ref,
    part_ref,
    stat_ref,
    cache_ref,
    turn_cos,
    turn_sin,
    wide,
    stats,
):
    me = lax.axis_index("tensor")
    f32 = jnp.float32
    bf16 = jnp.bfloat16
    total = (1 + STEPS) * count
    group = H // KVH
    q_dev, kv_dev = per_dev

    def q_head(h):
        return all_ref[h // q_dev, h % q_dev]

    def kv_head(j):
        return all_ref[j // kv_dev, q_dev + j % kv_dev]

    scale = 1.0 / math.sqrt(HD)
    row_ids = lax.broadcasted_iota(jnp.int32, (count, 1), 0)
    lens = jnp.zeros((count, 1), jnp.int32)
    for d in range(count):
        lens = jnp.where(row_ids == d, lens_ref[d], lens)
    offset = offset_ref[0]
    positions = jnp.concatenate([offset + row_ids] + [lens + t for t in range(STEPS)], axis=0)
    cos_part = jnp.ones((total, HD), f32)
    sin_part = jnp.zeros((total, HD), f32)
    for bit in range(rotation_bits):
        chosen = (positions >> bit & 1).astype(f32)
        step_cos = 1.0 + chosen * (cos_ref[bit : bit + 1, :] - 1.0)
        step_sin = chosen * sin_ref[bit : bit + 1, :]
        cos_part, sin_part = (
            cos_part * step_cos - sin_part * step_sin,
            sin_part * step_cos + cos_part * step_sin,
        )
    lanes = lax.broadcasted_iota(jnp.int32, (total, HD), 1)
    turn_cos[...] = cos_part
    turn_sin[...] = jnp.where(lanes < HD // 2, -sin_part, sin_part)

    def turn(x):
        wide_x = x.astype(f32)
        return (wide_x * turn_cos[...] + pltpu.roll(wide_x, HD // 2, 1) * turn_sin[...]).astype(bf16)

    prefix_dev = pk_ref.shape[0]
    slot = lax.broadcasted_iota(jnp.int32, (1, prefix_dev), 1)
    prefix_seen = me * prefix_dev + slot < offset

    pool_dev = dk_ref.shape[0]
    block_dev = pool_dev // PAGE
    token = lax.broadcasted_iota(jnp.int32, (1, pool_dev), 1)
    block_of = me * block_dev + token // PAGE
    entry_of = jnp.zeros((count, pool_dev), jnp.int32)
    for k in range(BLK_ROW):
        entry_of = jnp.where(map_ref[:, k : k + 1] == block_of, k + 1, entry_of)
    place = (entry_of - 1) * PAGE + token % PAGE
    live = (entry_of > 0) & (place < lens)
    key_row = jnp.sum(jnp.where(live, row_ids + 1, 0), axis=0, keepdims=True) - 1

    nh = heads_at_once
    span_q = lax.broadcasted_iota(jnp.int32, (nh * count, 1), 0) % count
    own_j = lax.broadcasted_iota(jnp.int32, (1, count), 1)
    span_own = (own_j == me) & (own_j <= span_q)
    dec_q = lax.broadcasted_iota(jnp.int32, (nh * STEPS * count, 1), 0)
    dec_row = dec_q % count
    dec_step = (dec_q // count) % STEPS
    new_j = lax.broadcasted_iota(jnp.int32, (1, STEPS * count), 1)
    dec_own = (new_j % count == me) & (dec_row == me) & (new_j // count <= dec_step)
    pick = lax.broadcasted_iota(jnp.int32, (count, 1), 0) == me
    stat_lane = lax.broadcasted_iota(jnp.int32, (count, 2 * H), 1)
    stats[...] = jnp.zeros_like(stats)
    stat_ref[...] = jnp.zeros_like(stat_ref)
    across = (((1,), (1,)), ((), ()))

    def soft(q, keys, values, seen, keys2, values2, seen2):
        s1 = lax.dot_general(q, keys, across, preferred_element_type=f32) * scale
        s2 = lax.dot_general(q, keys2, across, preferred_element_type=f32) * scale
        s1 = jnp.where(seen, s1, neg_fill)
        s2 = jnp.where(seen2, s2, neg_fill)
        top = jnp.maximum(
            jnp.max(s1, axis=1, keepdims=True), jnp.max(s2, axis=1, keepdims=True)
        )
        top = jnp.maximum(top, top_floor)
        w1 = jnp.exp(s1 - top)
        w2 = jnp.exp(s2 - top)
        den = jnp.sum(w1, axis=1, keepdims=True) + jnp.sum(w2, axis=1, keepdims=True)
        num = jnp.dot(w1.astype(bf16), values, preferred_element_type=f32) + jnp.dot(
            w2.astype(bf16), values2, preferred_element_type=f32
        )
        return top, den, num

    def per_head(g, carry):
        cols = pl.ds(pl.multiple_of(g * HD, HD), HD)
        new_keys = turn(kv_head(g))
        new_values = kv_head(KVH + g)
        cache_ref[pl.ds(g, 1), :] = jnp.sum(
            jnp.where(pick, new_keys[:count].astype(f32), 0.0), axis=0, keepdims=True
        )
        cache_ref[pl.ds(KVH + g, 1), :] = jnp.sum(
            jnp.where(pick, new_values[:count].astype(f32), 0.0), axis=0, keepdims=True
        )
        for first in range(0, group, nh):
            turned = [turn(q_head(g * group + first + i)) for i in range(nh)]
            span_queries = jnp.concatenate([t[:count] for t in turned], axis=0)
            dec_queries = jnp.concatenate([t[count:] for t in turned], axis=0)
            span_top, span_den, span_num = soft(
                span_queries,
                pk_ref[:, cols],
                pv_ref[:, cols],
                prefix_seen,
                new_keys[:count],
                new_values[:count],
                span_own,
            )
            dec_top, dec_den, dec_num = soft(
                dec_queries,
                dk_ref[:, cols],
                dv_ref[:, cols],
                key_row == dec_row,
                new_keys[count:],
                new_values[count:],
                dec_own,
            )
            for i in range(nh):
                head = g * group + first + i
                for kind in range(1 + STEPS):
                    if kind == 0:
                        rows = slice(i * count, (i + 1) * count)
                        top, den, num = span_top[rows], span_den[rows], span_num[rows]
                    else:
                        at = (i * STEPS + kind - 1) * count
                        rows = slice(at, at + count)
                        top, den, num = dec_top[rows], dec_den[rows], dec_num[rows]
                    wide[kind, pl.ds(head, count, stride=H), :] = num
                    stats[kind] = jnp.where(
                        stat_lane == head,
                        top,
                        jnp.where(stat_lane == H + head, den, stats[kind]),
                    )
        return carry

    lax.fori_loop(0, KVH, per_head, 0)
    for kind in range(1 + STEPS):
        stat_ref[pl.ds(kind, count, stride=8), :] = stats[kind]

    def pack(d, carry):
        for kind in range(1 + STEPS):
            rows = pl.ds(pl.multiple_of(d * H, H), H)
            part_ref[d, kind * H : (kind + 1) * H, :] = wide[kind, rows, :].astype(bf16)
        return carry

    lax.fori_loop(0, count, pack, 0)


def merge_kernel(count, part_ref, stat_ref, out_ref, parts, stats, send_sems, recv_sems, local_sems):
    me = lax.axis_index("tensor")
    f32 = jnp.float32
    sources, targets = (part_ref, stat_ref), (parts, stats)
    locals_ = [
        pltpu.make_async_copy(sources[a].at[me], targets[a].at[me], local_sems.at[a])
        for a in range(2)
    ]
    for copy in locals_:
        copy.start()
    greet_all(count, me)

    def remote(a, i):
        peer = lax.rem(me + i, count)
        return pltpu.make_async_remote_copy(
            src_ref=sources[a].at[peer],
            dst_ref=targets[a].at[me],
            send_sem=send_sems.at[a, i],
            recv_sem=recv_sems.at[a, i],
            device_id={"tensor": peer},
            device_id_type=pl.DeviceIdType.MESH,
        )

    def start(i, carry):
        for a in range(2):
            remote(a, i).start()
        return carry

    def finish(i, carry):
        for a in range(2):
            remote(a, i).wait()
        return carry

    lax.fori_loop(1, count, start, 0)
    for copy in locals_:
        copy.wait()
    lax.fori_loop(1, count, finish, 0)
    top = stats[0]
    for d in range(1, count):
        top = jnp.maximum(top, stats[d])
    den = jnp.zeros_like(top)
    for d in range(count):
        den = den + jnp.exp(stats[d] - top) * pltpu.roll(stats[d], H, 1)
    inverse = 1.0 / den
    share = jnp.concatenate([jnp.exp(stats[d] - top) * inverse for d in range(count)], axis=0).T
    for kind in range(1 + STEPS):
        acc = jnp.zeros((H, HD), f32)
        for d in range(count):
            acc = acc + share[:H, d * 8 + kind : d * 8 + kind + 1] * parts[
                d, kind * H : (kind + 1) * H, :
            ].astype(f32)
        out_ref[kind] = acc.astype(out_ref.dtype)


def shards(
    layout,
    span_rows,
    decode_rows,
    norm_gain,
    w_query,
    w_keyval,
    prefix_keys,
    prefix_values,
    span_offset,
    pool_keys,
    pool_values,
    row_blocks,
    context_lens,
):
    count = lax.axis_size("tensor")
    span_dev = span_rows.shape[0]
    rows_dev = decode_rows.shape[1]
    assert span_dev == 1 and rows_dev == 1
    kinds = 1 + STEPS
    total = kinds * count
    cut, kv_cols = w_query.shape[1], w_keyval.shape[1]
    heads = front(layout, span_rows, decode_rows, norm_gain, w_query, w_keyval)
    if heads.ndim == 4:
        q_dev, kv_dev = cut // HD, kv_cols // HD
    else:
        heads = heads.transpose(1, 0, 2)
        heads = jnp.concatenate(
            [heads[:, :, :cut].reshape(total, -1, HD), heads[:, :, cut:].reshape(total, -1, HD)],
            axis=1,
        ).transpose(1, 0, 2)[None]
        q_dev, kv_dev = H, 2 * KVH
    cos_table, sin_table = rotation_tables(HD // 2)
    tile = lambda x: jnp.concatenate([x, x], axis=1)
    part, stat, cache = pl.pallas_call(
        functools.partial(
            attend_kernel, count, H // KVH if count <= 32 else 1, (q_dev, kv_dev)
        ),
        out_shape=[
            jax.ShapeDtypeStruct((count, kinds * H, HD), jnp.bfloat16),
            jax.ShapeDtypeStruct((count * 8, 2 * H), jnp.float32),
            jax.ShapeDtypeStruct((2 * KVH, HD), jnp.float32),
        ],
        in_specs=[VMEM_SPEC] * 6
        + [pl.BlockSpec(memory_space=pltpu.SMEM)] * 2
        + [VMEM_SPEC] * 2,
        out_specs=[VMEM_SPEC] * 3,
        scratch_shapes=[
            pltpu.VMEM((total, HD), jnp.float32),
            pltpu.VMEM((total, HD), jnp.float32),
            pltpu.VMEM((kinds, count * H, HD), jnp.float32),
            pltpu.VMEM((kinds, count, 2 * H), jnp.float32),
        ],
        compiler_params=pltpu.CompilerParams(vmem_limit_bytes=VMEM_BYTES),
        name="attend",
    )(
        heads,
        prefix_keys,
        prefix_values,
        pool_keys.reshape(-1, KVH * HD),
        pool_values.reshape(-1, KVH * HD),
        row_blocks,
        span_offset,
        context_lens,
        tile(cos_table),
        tile(sin_table),
    )
    merged = pl.pallas_call(
        functools.partial(merge_kernel, count),
        out_shape=jax.ShapeDtypeStruct((kinds, H, HD), jnp.bfloat16),
        in_specs=[VMEM_SPEC] * 2,
        out_specs=VMEM_SPEC,
        scratch_shapes=[
            pltpu.VMEM((count, kinds * H, HD), jnp.bfloat16),
            pltpu.VMEM((count, 8, 2 * H), jnp.float32),
            pltpu.SemaphoreType.DMA((2, count)),
            pltpu.SemaphoreType.DMA((2, count)),
            pltpu.SemaphoreType.DMA((2,)),
        ],
        compiler_params=pltpu.CompilerParams(
            collective_id=2, has_side_effects=True, vmem_limit_bytes=VMEM_BYTES
        ),
        name="merge",
    )(part, stat.reshape(count, 8, 2 * H))
    span_attended = merged[0].reshape(1, D)
    decode_attended = merged[1:].reshape(STEPS, 1, D)
    span_cache = cache.reshape(1, 2 * KVH * HD).astype(jnp.bfloat16)
    return (span_attended, decode_attended, span_cache)


def solution(mesh):
    in_specs = (
        P(("groups", "tensor"), None),
        P(None, ("groups", "tensor"), None),
        P(),
        P(None, "tensor"),
        P(None, "tensor"),
        P(("groups", "tensor"), None),
        P(("groups", "tensor"), None),
        P("groups"),
        P(("groups", "tensor"), None, None),
        P(("groups", "tensor"), None, None),
        P("groups", None),
        P("groups"),
    )
    out_specs = (
        P(("groups", "tensor"), None),
        P(None, ("groups", "tensor"), None),
        P(("groups", "tensor"), None),
    )
    return jax.shard_map(
        functools.partial(shards, layout_of(mesh)),
        mesh=mesh,
        in_specs=in_specs,
        out_specs=out_specs,
        check_vma=False,
    )
```

```python
import functools
import math

import jax
import jax.numpy as jnp
import numpy as np
from jax import lax
from jax.experimental import pallas as pl
from jax.experimental.pallas import tpu as pltpu
from jax.sharding import PartitionSpec as P

D = 8192
H = 64
KVH = 8
HD = 128
PAGE = 16
STEPS = 2
BLK_ROW = 32


epsilon = 1e-05
neg_fill = -1e30
top_floor = -1e20
rotation_bits = 20


def llama_frequencies(half_width):
    exponents = np.arange(half_width) / (1.0 * half_width)
    inverse = 1.0 / 500000.0**exponents
    wavelen = 2.0 * np.pi / inverse
    scaled = np.where(wavelen > 8192.0, inverse / 8.0, inverse)
    smooth = (8192.0 / wavelen - 1.0) / 3.0
    blended = (1.0 - smooth) * inverse / 8.0 + smooth * inverse
    middle = (wavelen >= 2048.0) & (wavelen <= 8192.0)
    return np.where(middle, blended, scaled)


def rotation_tables(half_width):
    frequencies = llama_frequencies(half_width)
    powers = 2.0 ** np.arange(rotation_bits)
    angles = powers[:, None] * frequencies[None, :]
    return (jnp.asarray(np.cos(angles), jnp.float32), jnp.asarray(np.sin(angles), jnp.float32))


VMEM_BYTES = 60 * 1024 * 1024
VMEM_SPEC = pl.BlockSpec(memory_space=pltpu.VMEM)


def greet_all(count, me):
    barrier = pltpu.get_barrier_semaphore()

    def signal(i, carry):
        pl.semaphore_signal(
            barrier,
            inc=1,
            device_id={"tensor": lax.rem(me + i, count)},
            device_id_type=pl.DeviceIdType.MESH,
        )
        return carry

    lax.fori_loop(1, count, signal, 0)


def greet_near(layout):
    outer, inner, cores = layout
    me = lax.axis_index("tensor")
    core = lax.rem(me, cores)
    column = lax.rem(me // cores, inner)
    plane = me // (cores * inner)
    peers = [(lax.rem(plane + i, outer) * inner + column) * cores + core for i in range(1, outer)]
    peers += [(plane * inner + lax.rem(column + i, inner)) * cores + core for i in range(1, inner)]
    peers += [(plane * inner + column) * cores + lax.rem(core + i, cores) for i in range(1, cores)]
    barrier = pltpu.get_barrier_semaphore()
    for peer in peers:
        pl.semaphore_signal(
            barrier,
            inc=1,
            device_id={"tensor": peer},
            device_id_type=pl.DeviceIdType.MESH,
        )
    pl.semaphore_wait(barrier, len(peers))


def layout_of(mesh):
    count = mesh.shape["tensor"]
    line = mesh.devices.reshape(-1, count)[0]
    coords = [tuple(getattr(device, "coords", (i,))) for i, device in enumerate(line)]
    cores = sum(1 for c in coords if c == coords[0])
    chips = coords[::cores]
    inner = 1
    if len(chips) > 1:
        axis = [p != q for p, q in zip(chips[0], chips[1])].index(True)
        inner = len({c[axis] for c in chips})
    if count % (cores * inner):
        return count, 1, 1
    return count // (cores * inner), inner, cores


def spread_copies(layout, target, send_sems, recv_sems):
    outer, inner, cores = layout
    me = lax.axis_index("tensor")
    core = lax.rem(me, cores)
    column = lax.rem(me // cores, inner)
    plane = me // (cores * inner)
    pending = []
    source = target.at[me]

    def index(z, y, c):
        return (z * inner + y) * cores + c

    def send(owner, src, peer, slot):
        copy = pltpu.make_async_remote_copy(
            src_ref=src,
            dst_ref=target.at[owner],
            send_sem=send_sems.at[slot],
            recv_sem=recv_sems.at[owner],
            device_id={"tensor": peer},
            device_id_type=pl.DeviceIdType.MESH,
        )
        copy.start()
        pending.append(copy)

    def arrived(owner):
        pltpu.make_async_remote_copy(
            src_ref=source,
            dst_ref=target.at[owner],
            send_sem=send_sems.at[0],
            recv_sem=recv_sems.at[owner],
            device_id={"tensor": index(plane, column, lax.rem(core + 1, cores))},
            device_id_type=pl.DeviceIdType.MESH,
        ).wait_recv()

    slots = iter(range(outer * inner * cores))
    for i in range(1, outer):
        send(me, source, index(lax.rem(plane + i, outer), column, core), next(slots))
    for j in range(outer):
        owner = index(lax.rem(plane + outer - j, outer), column, core)
        if j > 0:
            arrived(owner)
        src = source if j == 0 else target.at[owner]
        for k in range(1, inner):
            send(owner, src, index(plane, lax.rem(column + k, inner), core), next(slots))
        for k in range(1, cores):
            send(owner, src, index(plane, column, lax.rem(core + k, cores)), next(slots))
    for j in range(outer):
        for k in range(1, inner):
            owner = index(
                lax.rem(plane + outer - j, outer), lax.rem(column + inner - k, inner), core
            )
            arrived(owner)
            for n in range(1, cores):
                peer = index(plane, column, lax.rem(core + n, cores))
                send(owner, target.at[owner], peer, next(slots))
    for j in range(outer):
        for k in range(inner):
            for n in range(1, cores):
                arrived(
                    index(
                        lax.rem(plane + outer - j, outer),
                        lax.rem(column + inner - k, inner),
                        lax.rem(core + cores - n, cores),
                    )
                )
    for copy in pending:
        copy.wait_send()


def front_kernel(
    layout,
    span_ref,
    decode_ref,
    gain_ref,
    wq_hbm,
    wkv_hbm,
    heads_ref,
    lines,
    gathered,
    spread_rows,
    wq_buf,
    wkv_buf,
    weight_sems,
    send_sems,
    recv_sems,
    send_sems2,
    recv_sems2,
):
    f32 = jnp.float32
    count = math.prod(layout)
    me = lax.axis_index("tensor")
    depth, pieces = wq_hbm.shape[0], weight_sems.shape[1]
    step = depth // pieces
    fetches = []
    for i in range(pieces):
        rows = pl.ds(i * step, step)
        for a, (src, dst) in enumerate(((wq_hbm, wq_buf), (wkv_hbm, wkv_buf))):
            copy = pltpu.make_async_copy(src.at[rows], dst.at[rows], weight_sems.at[a, i])
            copy.start()
            fetches.append(copy)
    gain = gain_ref[...].astype(f32)
    width = lines.shape[1]
    folds = depth // width
    kinds = lines.shape[0] // folds
    for first, ref in ((0, span_ref), (1, decode_ref)):
        x = ref[...].astype(f32)
        mean_square = jnp.mean(x * x, axis=-1, keepdims=True)
        x = x * lax.rsqrt(mean_square + epsilon) * gain
        for r in range(x.shape[0]):
            for k in range(folds):
                lines[pl.ds((first + r) * folds + k, 1), :] = x[
                    r : r + 1, k * width : (k + 1) * width
                ]
    gathered[me] = lines[...].astype(jnp.bfloat16)
    greet_near(layout)
    spread_copies(layout, gathered, send_sems, recv_sems)

    def widen(d, carry):
        rows = pl.ds(pl.multiple_of(d * kinds * folds, kinds * folds), kinds * folds)
        for j in range(width // HD):
            spread_rows[j, rows, :] = gathered[d, :, j * HD : (j + 1) * HD].astype(f32)
        return carry

    lax.fori_loop(0, count, widen, 0)
    total = kinds * count
    queries = jnp.zeros((total, wq_hbm.shape[1]), f32)
    keyval = jnp.zeros((total, wkv_hbm.shape[1]), f32)
    for k in range(folds):
        if k * width % step == 0:
            at = k * width // step
            fetches[2 * at].wait()
            fetches[2 * at + 1].wait()
        rows = jnp.concatenate(
            [
                jnp.concatenate(
                    [
                        spread_rows[j, pl.ds(kind * folds + k, count, stride=kinds * folds), :]
                        for kind in range(kinds)
                    ],
                    axis=0,
                )
                for j in range(width // HD)
            ],
            axis=1,
        ).astype(jnp.bfloat16)
        part = slice(k * width, (k + 1) * width)
        queries += jnp.dot(rows, wq_buf[part, :], preferred_element_type=f32)
        keyval += jnp.dot(rows, wkv_buf[part, :], preferred_element_type=f32)
    if len(heads_ref.shape) == 4:
        q_dev = queries.shape[1] // HD
        for h in range(heads_ref.shape[1]):
            x = queries if h < q_dev else keyval
            at = (h if h < q_dev else h - q_dev) * HD
            heads_ref[me, h] = x[:, at : at + HD].astype(jnp.bfloat16)
    else:
        heads_ref[me] = jnp.concatenate([queries, keyval], axis=1).astype(jnp.bfloat16)
    spread_copies(layout, heads_ref, send_sems2, recv_sems2)


def front(layout, span_rows, decode_rows, norm_gain, w_query, w_keyval):
    count = math.prod(layout)
    kinds = 1 + STEPS
    total = kinds * count
    depth, q_cols = w_query.shape
    kv_cols = w_keyval.shape[1]
    width = 512
    by_head = q_cols % HD == 0 and kv_cols % HD == 0
    heads = ((q_cols + kv_cols) // HD, total, HD) if by_head else (total, q_cols + kv_cols)
    dma = pltpu.SemaphoreType.DMA
    return pl.pallas_call(
        functools.partial(front_kernel, layout),
        out_shape=jax.ShapeDtypeStruct((count,) + heads, jnp.bfloat16),
        in_specs=[VMEM_SPEC] * 3 + [pl.BlockSpec(memory_space=pl.ANY)] * 2,
        out_specs=VMEM_SPEC,
        scratch_shapes=[
            pltpu.VMEM((kinds * depth // width, width), jnp.float32),
            pltpu.VMEM((count, kinds * depth // width, width), jnp.bfloat16),
            pltpu.VMEM((width // HD, count * kinds * depth // width, HD), jnp.float32),
            pltpu.VMEM(w_query.shape, jnp.bfloat16),
            pltpu.VMEM(w_keyval.shape, jnp.bfloat16),
            dma((2, 4)),
            dma((count,)),
            dma((count,)),
            dma((count,)),
            dma((count,)),
        ],
        compiler_params=pltpu.CompilerParams(
            collective_id=0, has_side_effects=True, vmem_limit_bytes=VMEM_BYTES
        ),
        name="front",
    )(span_rows, decode_rows.reshape(STEPS, depth), norm_gain.reshape(1, depth), w_query, w_keyval)


def attend_kernel(
    count,
    heads_at_once,
    per_dev,
    all_ref,
    pk_ref,
    pv_ref,
    dk_ref,
    dv_ref,
    map_ref,
    offset_ref,
    lens_ref,
    cos_ref,
    sin_ref,
    span_out,
    decode_out,
    cache_out,
    turn_cos,
    turn_sin,
    wide,
    stats,
    cache_ref,
    own_parts,
    own_stats,
    parts,
    all_stats,
    send_sems,
    recv_sems,
    local_sems,
):
    me = lax.axis_index("tensor")
    greet_all(count, me)
    f32 = jnp.float32
    bf16 = jnp.bfloat16
    total = (1 + STEPS) * count
    group = H // KVH
    q_dev, kv_dev = per_dev

    def q_head(h):
        return all_ref[h // q_dev, h % q_dev]

    def kv_head(j):
        return all_ref[j // kv_dev, q_dev + j % kv_dev]

    scale = 1.0 / math.sqrt(HD)
    row_ids = lax.broadcasted_iota(jnp.int32, (count, 1), 0)
    lens = jnp.zeros((count, 1), jnp.int32)
    for d in range(count):
        lens = jnp.where(row_ids == d, lens_ref[d], lens)
    offset = offset_ref[0]
    positions = jnp.concatenate([offset + row_ids] + [lens + t for t in range(STEPS)], axis=0)
    cos_part = jnp.ones((total, HD), f32)
    sin_part = jnp.zeros((total, HD), f32)
    for bit in range(rotation_bits):
        chosen = (positions >> bit & 1).astype(f32)
        step_cos = 1.0 + chosen * (cos_ref[bit : bit + 1, :] - 1.0)
        step_sin = chosen * sin_ref[bit : bit + 1, :]
        cos_part, sin_part = (
            cos_part * step_cos - sin_part * step_sin,
            sin_part * step_cos + cos_part * step_sin,
        )
    lanes = lax.broadcasted_iota(jnp.int32, (total, HD), 1)
    turn_cos[...] = cos_part
    turn_sin[...] = jnp.where(lanes < HD // 2, -sin_part, sin_part)

    def turn(x):
        wide_x = x.astype(f32)
        return (wide_x * turn_cos[...] + pltpu.roll(wide_x, HD // 2, 1) * turn_sin[...]).astype(bf16)

    prefix_dev = pk_ref.shape[0]
    slot = lax.broadcasted_iota(jnp.int32, (1, prefix_dev), 1)
    prefix_seen = me * prefix_dev + slot < offset

    pool_dev = dk_ref.shape[0]
    block_dev = pool_dev // PAGE
    token = lax.broadcasted_iota(jnp.int32, (1, pool_dev), 1)
    block_of = me * block_dev + token // PAGE
    entry_of = jnp.zeros((count, pool_dev), jnp.int32)
    for k in range(BLK_ROW):
        entry_of = jnp.where(map_ref[:, k : k + 1] == block_of, k + 1, entry_of)
    place = (entry_of - 1) * PAGE + token % PAGE
    live = (entry_of > 0) & (place < lens)
    key_row = jnp.sum(jnp.where(live, row_ids + 1, 0), axis=0, keepdims=True) - 1

    nh = heads_at_once
    span_q = lax.broadcasted_iota(jnp.int32, (nh * count, 1), 0) % count
    own_j = lax.broadcasted_iota(jnp.int32, (1, count), 1)
    span_own = (own_j == me) & (own_j <= span_q)
    dec_q = lax.broadcasted_iota(jnp.int32, (nh * STEPS * count, 1), 0)
    dec_row = dec_q % count
    dec_step = (dec_q // count) % STEPS
    new_j = lax.broadcasted_iota(jnp.int32, (1, STEPS * count), 1)
    dec_own = (new_j % count == me) & (dec_row == me) & (new_j // count <= dec_step)
    pick = lax.broadcasted_iota(jnp.int32, (count, 1), 0) == me
    stat_lane = lax.broadcasted_iota(jnp.int32, (count, 2 * H), 1)
    stats[...] = jnp.zeros_like(stats)
    own_stats[...] = jnp.zeros_like(own_stats)
    across = (((1,), (1,)), ((), ()))

    def soft(q, keys, values, seen, keys2, values2, seen2):
        s1 = lax.dot_general(q, keys, across, preferred_element_type=f32) * scale
        s2 = lax.dot_general(q, keys2, across, preferred_element_type=f32) * scale
        s1 = jnp.where(seen, s1, neg_fill)
        s2 = jnp.where(seen2, s2, neg_fill)
        top = jnp.maximum(
            jnp.max(s1, axis=1, keepdims=True), jnp.max(s2, axis=1, keepdims=True)
        )
        top = jnp.maximum(top, top_floor)
        w1 = jnp.exp(s1 - top)
        w2 = jnp.exp(s2 - top)
        den = jnp.sum(w1, axis=1, keepdims=True) + jnp.sum(w2, axis=1, keepdims=True)
        num = jnp.dot(w1.astype(bf16), values, preferred_element_type=f32) + jnp.dot(
            w2.astype(bf16), values2, preferred_element_type=f32
        )
        return top, den, num

    kinds = 1 + STEPS

    def part_copy(i, g):
        peer = lax.rem(me + i, count)
        return pltpu.make_async_remote_copy(
            src_ref=own_parts.at[peer, g],
            dst_ref=parts.at[me, g],
            send_sem=send_sems.at[0, i],
            recv_sem=recv_sems.at[0, i],
            device_id={"tensor": peer},
            device_id_type=pl.DeviceIdType.MESH,
        )

    def all_parts(i):
        return pltpu.make_async_remote_copy(
            src_ref=own_parts.at[lax.rem(me + i, count)],
            dst_ref=parts.at[lax.rem(me + count - i, count)],
            send_sem=send_sems.at[0, i],
            recv_sem=recv_sems.at[0, i],
            device_id={"tensor": lax.rem(me + i, count)},
            device_id_type=pl.DeviceIdType.MESH,
        )

    def stat_copy(i):
        peer = lax.rem(me + i, count)
        return pltpu.make_async_remote_copy(
            src_ref=own_stats.at[pl.ds(pl.multiple_of(peer * 8, 8), 8)],
            dst_ref=all_stats.at[me],
            send_sem=send_sems.at[1, i],
            recv_sem=recv_sems.at[1, i],
            device_id={"tensor": peer},
            device_id_type=pl.DeviceIdType.MESH,
        )

    pl.semaphore_wait(pltpu.get_barrier_semaphore(), count - 1)

    def per_head(g, carry):
        cols = pl.ds(pl.multiple_of(g * HD, HD), HD)
        new_keys = turn(kv_head(g))
        new_values = kv_head(KVH + g)
        cache_ref[pl.ds(g, 1), :] = jnp.sum(
            jnp.where(pick, new_keys[:count].astype(f32), 0.0), axis=0, keepdims=True
        )
        cache_ref[pl.ds(KVH + g, 1), :] = jnp.sum(
            jnp.where(pick, new_values[:count].astype(f32), 0.0), axis=0, keepdims=True
        )
        for first in range(0, group, nh):
            turned = [turn(q_head(g * group + first + i)) for i in range(nh)]
            span_queries = jnp.concatenate([t[:count] for t in turned], axis=0)
            dec_queries = jnp.concatenate([t[count:] for t in turned], axis=0)
            span_top, span_den, span_num = soft(
                span_queries,
                pk_ref[:, cols],
                pv_ref[:, cols],
                prefix_seen,
                new_keys[:count],
                new_values[:count],
                span_own,
            )
            dec_top, dec_den, dec_num = soft(
                dec_queries,
                dk_ref[:, cols],
                dv_ref[:, cols],
                key_row == dec_row,
                new_keys[count:],
                new_values[count:],
                dec_own,
            )
            for i in range(nh):
                head = g * group + first + i
                for kind in range(1 + STEPS):
                    if kind == 0:
                        rows = slice(i * count, (i + 1) * count)
                        top, den, num = span_top[rows], span_den[rows], span_num[rows]
                    else:
                        at = (i * STEPS + kind - 1) * count
                        rows = slice(at, at + count)
                        top, den, num = dec_top[rows], dec_den[rows], dec_num[rows]
                    wide[pl.ds(kind * group + first + i, count, stride=kinds * group), :] = num
                    stats[kind] = jnp.where(
                        stat_lane == head,
                        top,
                        jnp.where(stat_lane == H + head, den, stats[kind]),
                    )

        def pack(d, carry):
            rows = pl.ds(pl.multiple_of(d * kinds * group, kinds * group), kinds * group)
            own_parts[d, g] = wide[rows, :].astype(bf16)
            return carry

        def send(i, carry):
            part_copy(i, g).start()
            return carry

        lax.fori_loop(0, count, pack, 0)
        lax.fori_loop(1, count, send, 0)
        return carry

    lax.fori_loop(0, KVH, per_head, 0)
    for kind in range(kinds):
        own_stats[pl.ds(kind, count, stride=8), :] = stats[kind]

    def send_stats(i, carry):
        stat_copy(i).start()
        return carry

    lax.fori_loop(1, count, send_stats, 0)
    own = (
        pltpu.make_async_copy(own_parts.at[me], parts.at[me], local_sems.at[0]),
        pltpu.make_async_copy(
            own_stats.at[pl.ds(pl.multiple_of(me * 8, 8), 8)], all_stats.at[me], local_sems.at[1]
        ),
    )
    for copy in own:
        copy.start()
    for j in range(2 * KVH):
        cache_out[0:1, j * HD : (j + 1) * HD] = cache_ref[j : j + 1, :].astype(cache_out.dtype)
    for copy in own:
        copy.wait()

    def finish(i, carry):
        all_parts(i).wait()
        stat_copy(i).wait()
        return carry

    lax.fori_loop(1, count, finish, 0)
    best = all_stats[0]
    for d in range(1, count):
        best = jnp.maximum(best, all_stats[d])
    den = jnp.zeros_like(best)
    for d in range(count):
        den = den + jnp.exp(all_stats[d] - best) * pltpu.roll(all_stats[d], H, 1)
    inverse = 1.0 / den
    share = jnp.concatenate(
        [jnp.exp(all_stats[d] - best) * inverse for d in range(count)], axis=0
    ).T
    sums = [jnp.zeros((H, HD), f32) for _ in range(kinds)]
    for d in range(count):
        arrived = parts[d].astype(f32)
        for kind in range(kinds):
            rows = arrived[:, kind * group : (kind + 1) * group, :].reshape(H, HD)
            sums[kind] = sums[kind] + share[:H, d * 8 + kind : d * 8 + kind + 1] * rows
    for h in range(H):
        cols = slice(h * HD, (h + 1) * HD)
        span_out[0:1, cols] = sums[0][h : h + 1, :].astype(span_out.dtype)
        for t in range(STEPS):
            decode_out[t : t + 1, cols] = sums[1 + t][h : h + 1, :].astype(decode_out.dtype)


def shards(
    layout,
    span_rows,
    decode_rows,
    norm_gain,
    w_query,
    w_keyval,
    prefix_keys,
    prefix_values,
    span_offset,
    pool_keys,
    pool_values,
    row_blocks,
    context_lens,
):
    count = lax.axis_size("tensor")
    span_dev = span_rows.shape[0]
    rows_dev = decode_rows.shape[1]
    assert span_dev == 1 and rows_dev == 1
    kinds = 1 + STEPS
    total = kinds * count
    cut, kv_cols = w_query.shape[1], w_keyval.shape[1]
    heads = front(layout, span_rows, decode_rows, norm_gain, w_query, w_keyval)
    if heads.ndim == 4:
        q_dev, kv_dev = cut // HD, kv_cols // HD
    else:
        heads = heads.transpose(1, 0, 2)
        heads = jnp.concatenate(
            [heads[:, :, :cut].reshape(total, -1, HD), heads[:, :, cut:].reshape(total, -1, HD)],
            axis=1,
        ).transpose(1, 0, 2)[None]
        q_dev, kv_dev = H, 2 * KVH
    cos_table, sin_table = rotation_tables(HD // 2)
    tile = lambda x: jnp.concatenate([x, x], axis=1)
    dma = pltpu.SemaphoreType.DMA
    span_attended, decode_attended, span_cache = pl.pallas_call(
        functools.partial(
            attend_kernel, count, H // KVH if count <= 32 else 1, (q_dev, kv_dev)
        ),
        out_shape=[
            jax.ShapeDtypeStruct((1, D), jnp.bfloat16),
            jax.ShapeDtypeStruct((STEPS, D), jnp.bfloat16),
            jax.ShapeDtypeStruct((1, 2 * KVH * HD), jnp.bfloat16),
        ],
        in_specs=[VMEM_SPEC] * 6
        + [pl.BlockSpec(memory_space=pltpu.SMEM)] * 2
        + [VMEM_SPEC] * 2,
        out_specs=[VMEM_SPEC] * 3,
        scratch_shapes=[
            pltpu.VMEM((total, HD), jnp.float32),
            pltpu.VMEM((total, HD), jnp.float32),
            pltpu.VMEM((count * kinds * H // KVH, HD), jnp.float32),
            pltpu.VMEM((kinds, count, 2 * H), jnp.float32),
            pltpu.VMEM((2 * KVH, HD), jnp.float32),
            pltpu.VMEM((count, KVH, kinds * H // KVH, HD), jnp.bfloat16),
            pltpu.VMEM((count * 8, 2 * H), jnp.float32),
            pltpu.VMEM((count, KVH, kinds * H // KVH, HD), jnp.bfloat16),
            pltpu.VMEM((count, 8, 2 * H), jnp.float32),
            dma((2, count)),
            dma((2, count)),
            dma((2,)),
        ],
        compiler_params=pltpu.CompilerParams(
            collective_id=1, has_side_effects=True, vmem_limit_bytes=VMEM_BYTES
        ),
        name="attend",
    )(
        heads,
        prefix_keys,
        prefix_values,
        pool_keys.reshape(-1, KVH * HD),
        pool_values.reshape(-1, KVH * HD),
        row_blocks,
        span_offset,
        context_lens,
        tile(cos_table),
        tile(sin_table),
    )
    decode_attended = decode_attended.reshape(STEPS, 1, D)
    return (span_attended, decode_attended, span_cache)


def solution(mesh):
    in_specs = (
        P(("groups", "tensor"), None),
        P(None, ("groups", "tensor"), None),
        P(),
        P(None, "tensor"),
        P(None, "tensor"),
        P(("groups", "tensor"), None),
        P(("groups", "tensor"), None),
        P("groups"),
        P(("groups", "tensor"), None, None),
        P(("groups", "tensor"), None, None),
        P("groups", None),
        P("groups"),
    )
    out_specs = (
        P(("groups", "tensor"), None),
        P(None, ("groups", "tensor"), None),
        P(("groups", "tensor"), None),
    )
    return jax.shard_map(
        functools.partial(shards, layout_of(mesh)),
        mesh=mesh,
        in_specs=in_specs,
        out_specs=out_specs,
        check_vma=False,
    )
```

```python
import functools
import math

import jax
import jax.numpy as jnp
import numpy as np
from jax import lax
from jax.experimental import pallas as pl
from jax.experimental.pallas import tpu as pltpu
from jax.sharding import PartitionSpec as P

D = 8192
H = 64
KVH = 8
HD = 128
PAGE = 16
STEPS = 2
BLK_ROW = 32


epsilon = 1e-05
neg_fill = -1e30
top_floor = -1e20
rotation_bits = 20


def llama_frequencies(half_width):
    exponents = np.arange(half_width) / (1.0 * half_width)
    inverse = 1.0 / 500000.0**exponents
    wavelen = 2.0 * np.pi / inverse
    scaled = np.where(wavelen > 8192.0, inverse / 8.0, inverse)
    smooth = (8192.0 / wavelen - 1.0) / 3.0
    blended = (1.0 - smooth) * inverse / 8.0 + smooth * inverse
    middle = (wavelen >= 2048.0) & (wavelen <= 8192.0)
    return np.where(middle, blended, scaled)


def rotation_tables(half_width):
    frequencies = llama_frequencies(half_width)
    powers = 2.0 ** np.arange(rotation_bits)
    angles = powers[:, None] * frequencies[None, :]
    return (jnp.asarray(np.cos(angles), jnp.float32), jnp.asarray(np.sin(angles), jnp.float32))


VMEM_BYTES = 60 * 1024 * 1024
VMEM_SPEC = pl.BlockSpec(memory_space=pltpu.VMEM)


def greet_all(count, me):
    barrier = pltpu.get_barrier_semaphore()

    def signal(i, carry):
        pl.semaphore_signal(
            barrier,
            inc=1,
            device_id={"tensor": lax.rem(me + i, count)},
            device_id_type=pl.DeviceIdType.MESH,
        )
        return carry

    lax.fori_loop(1, count, signal, 0)


def greet_near(layout):
    outer, inner, cores = layout
    me = lax.axis_index("tensor")
    core = lax.rem(me, cores)
    column = lax.rem(me // cores, inner)
    plane = me // (cores * inner)
    peers = [(lax.rem(plane + i, outer) * inner + column) * cores + core for i in range(1, outer)]
    peers += [(plane * inner + lax.rem(column + i, inner)) * cores + core for i in range(1, inner)]
    peers += [(plane * inner + column) * cores + lax.rem(core + i, cores) for i in range(1, cores)]
    barrier = pltpu.get_barrier_semaphore()
    for peer in peers:
        pl.semaphore_signal(
            barrier,
            inc=1,
            device_id={"tensor": peer},
            device_id_type=pl.DeviceIdType.MESH,
        )
    pl.semaphore_wait(barrier, len(peers))


def layout_of(mesh):
    count = mesh.shape["tensor"]
    line = mesh.devices.reshape(-1, count)[0]
    coords = [tuple(getattr(device, "coords", (i,))) for i, device in enumerate(line)]
    cores = sum(1 for c in coords if c == coords[0])
    chips = coords[::cores]
    inner = 1
    if len(chips) > 1:
        axis = [p != q for p, q in zip(chips[0], chips[1])].index(True)
        inner = len({c[axis] for c in chips})
    if count % (cores * inner):
        return count, 1, 1
    return count // (cores * inner), inner, cores


def spread_copies(layout, target, send_sems, recv_sems):
    outer, inner, cores = layout
    me = lax.axis_index("tensor")
    core = lax.rem(me, cores)
    column = lax.rem(me // cores, inner)
    plane = me // (cores * inner)
    pending = []
    source = target.at[me]

    def index(z, y, c):
        return (z * inner + y) * cores + c

    def send(owner, src, peer, slot):
        copy = pltpu.make_async_remote_copy(
            src_ref=src,
            dst_ref=target.at[owner],
            send_sem=send_sems.at[slot],
            recv_sem=recv_sems.at[owner],
            device_id={"tensor": peer},
            device_id_type=pl.DeviceIdType.MESH,
        )
        copy.start()
        pending.append(copy)

    def arrived(owner):
        pltpu.make_async_remote_copy(
            src_ref=source,
            dst_ref=target.at[owner],
            send_sem=send_sems.at[0],
            recv_sem=recv_sems.at[owner],
            device_id={"tensor": index(plane, column, lax.rem(core + 1, cores))},
            device_id_type=pl.DeviceIdType.MESH,
        ).wait_recv()

    slots = iter(range(outer * inner * cores))
    near = sorted(range(outer), key=lambda i: min(i, outer - i))
    for i in near[1:]:
        send(me, source, index(lax.rem(plane + i, outer), column, core), next(slots))
    for j in near:
        owner = index(lax.rem(plane + outer - j, outer), column, core)
        if j > 0:
            arrived(owner)
        src = source if j == 0 else target.at[owner]
        for k in range(1, inner):
            send(owner, src, index(plane, lax.rem(column + k, inner), core), next(slots))
        for k in range(1, cores):
            send(owner, src, index(plane, column, lax.rem(core + k, cores)), next(slots))
    for j in near:
        for k in range(1, inner):
            owner = index(
                lax.rem(plane + outer - j, outer), lax.rem(column + inner - k, inner), core
            )
            arrived(owner)
            for n in range(1, cores):
                peer = index(plane, column, lax.rem(core + n, cores))
                send(owner, target.at[owner], peer, next(slots))
    for j in range(outer):
        for k in range(inner):
            for n in range(1, cores):
                arrived(
                    index(
                        lax.rem(plane + outer - j, outer),
                        lax.rem(column + inner - k, inner),
                        lax.rem(core + cores - n, cores),
                    )
                )
    for copy in pending:
        copy.wait_send()


def front_kernel(
    layout,
    span_ref,
    decode_ref,
    gain_ref,
    wq_hbm,
    wkv_hbm,
    heads_ref,
    lines,
    gathered,
    spread_rows,
    wq_buf,
    wkv_buf,
    weight_sems,
    send_sems,
    recv_sems,
    send_sems2,
    recv_sems2,
):
    f32 = jnp.float32
    count = math.prod(layout)
    me = lax.axis_index("tensor")
    depth, pieces = wq_hbm.shape[0], weight_sems.shape[1]
    step = depth // pieces
    fetches = []
    for i in range(pieces):
        rows = pl.ds(i * step, step)
        for a, (src, dst) in enumerate(((wq_hbm, wq_buf), (wkv_hbm, wkv_buf))):
            copy = pltpu.make_async_copy(src.at[rows], dst.at[rows], weight_sems.at[a, i])
            copy.start()
            fetches.append(copy)
    gain = gain_ref[...].astype(f32).reshape(1, depth)
    width = lines.shape[1]
    folds = depth // width
    kinds = lines.shape[0] // folds
    for first, ref in ((0, span_ref), (1, decode_ref)):
        x = ref[...].astype(f32)
        mean_square = jnp.mean(x * x, axis=-1, keepdims=True)
        x = x * lax.rsqrt(mean_square + epsilon) * gain
        for r in range(x.shape[0]):
            for k in range(folds):
                lines[pl.ds((first + r) * folds + k, 1), :] = x[
                    r : r + 1, k * width : (k + 1) * width
                ]
    gathered[me] = lines[...].astype(jnp.bfloat16)
    greet_near(layout)
    spread_copies(layout, gathered, send_sems, recv_sems)

    def widen(d, carry):
        rows = pl.ds(pl.multiple_of(d * kinds * folds, kinds * folds), kinds * folds)
        for j in range(width // HD):
            spread_rows[j, rows, :] = gathered[d, :, j * HD : (j + 1) * HD].astype(f32)
        return carry

    lax.fori_loop(0, count, widen, 0)
    total = kinds * count
    queries = jnp.zeros((total, wq_hbm.shape[1]), f32)
    keyval = jnp.zeros((total, wkv_hbm.shape[1]), f32)
    for k in range(folds):
        if k * width % step == 0:
            at = k * width // step
            fetches[2 * at].wait()
            fetches[2 * at + 1].wait()
        rows = jnp.concatenate(
            [
                jnp.concatenate(
                    [
                        spread_rows[j, pl.ds(kind * folds + k, count, stride=kinds * folds), :]
                        for kind in range(kinds)
                    ],
                    axis=0,
                )
                for j in range(width // HD)
            ],
            axis=1,
        ).astype(jnp.bfloat16)
        part = slice(k * width, (k + 1) * width)
        queries += jnp.dot(rows, wq_buf[part, :], preferred_element_type=f32)
        keyval += jnp.dot(rows, wkv_buf[part, :], preferred_element_type=f32)
    if len(heads_ref.shape) == 4:
        q_dev = queries.shape[1] // HD
        for h in range(heads_ref.shape[1]):
            x = queries if h < q_dev else keyval
            at = (h if h < q_dev else h - q_dev) * HD
            heads_ref[me, h] = x[:, at : at + HD].astype(jnp.bfloat16)
    else:
        heads_ref[me] = jnp.concatenate([queries, keyval], axis=1).astype(jnp.bfloat16)
    spread_copies(layout, heads_ref, send_sems2, recv_sems2)


def front(layout, span_rows, decode_rows, norm_gain, w_query, w_keyval):
    count = math.prod(layout)
    kinds = 1 + STEPS
    total = kinds * count
    depth, q_cols = w_query.shape
    kv_cols = w_keyval.shape[1]
    width = 512
    by_head = q_cols % HD == 0 and kv_cols % HD == 0
    heads = ((q_cols + kv_cols) // HD, total, HD) if by_head else (total, q_cols + kv_cols)
    dma = pltpu.SemaphoreType.DMA
    return pl.pallas_call(
        functools.partial(front_kernel, layout),
        out_shape=jax.ShapeDtypeStruct((count,) + heads, jnp.bfloat16),
        in_specs=[VMEM_SPEC] * 3 + [pl.BlockSpec(memory_space=pl.ANY)] * 2,
        out_specs=VMEM_SPEC,
        scratch_shapes=[
            pltpu.VMEM((kinds * depth // width, width), jnp.float32),
            pltpu.VMEM((count, kinds * depth // width, width), jnp.bfloat16),
            pltpu.VMEM((width // HD, count * kinds * depth // width, HD), jnp.float32),
            pltpu.VMEM(w_query.shape, jnp.bfloat16),
            pltpu.VMEM(w_keyval.shape, jnp.bfloat16),
            dma((2, 4)),
            dma((count,)),
            dma((count,)),
            dma((count,)),
            dma((count,)),
        ],
        compiler_params=pltpu.CompilerParams(
            collective_id=0, has_side_effects=True, vmem_limit_bytes=VMEM_BYTES
        ),
        name="front",
    )(span_rows, decode_rows.reshape(STEPS, depth), norm_gain, w_query, w_keyval)


def attend_kernel(
    count,
    heads_at_once,
    per_dev,
    all_ref,
    pk_ref,
    pv_ref,
    dk_ref,
    dv_ref,
    map_ref,
    offset_ref,
    lens_ref,
    cos_ref,
    sin_ref,
    span_out,
    decode_out,
    cache_out,
    turn_cos,
    turn_sin,
    wide,
    stats,
    cache_ref,
    own_parts,
    own_stats,
    parts,
    all_stats,
    send_sems,
    recv_sems,
    local_sems,
):
    me = lax.axis_index("tensor")
    greet_all(count, me)
    f32 = jnp.float32
    bf16 = jnp.bfloat16
    total = (1 + STEPS) * count
    group = H // KVH
    q_dev, kv_dev = per_dev

    def q_head(h):
        return all_ref[h // q_dev, h % q_dev]

    def kv_head(j):
        return all_ref[j // kv_dev, q_dev + j % kv_dev]

    scale = 1.0 / math.sqrt(HD)
    row_ids = lax.broadcasted_iota(jnp.int32, (count, 1), 0)
    lens = jnp.zeros((count, 1), jnp.int32)
    for d in range(count):
        lens = jnp.where(row_ids == d, lens_ref[d], lens)
    offset = offset_ref[0]
    positions = jnp.concatenate([offset + row_ids] + [lens + t for t in range(STEPS)], axis=0)
    cos_part = jnp.ones((total, HD), f32)
    sin_part = jnp.zeros((total, HD), f32)
    for bit in range(rotation_bits):
        chosen = (positions >> bit & 1).astype(f32)
        step_cos = 1.0 + chosen * (cos_ref[bit : bit + 1, :] - 1.0)
        step_sin = chosen * sin_ref[bit : bit + 1, :]
        cos_part, sin_part = (
            cos_part * step_cos - sin_part * step_sin,
            sin_part * step_cos + cos_part * step_sin,
        )
    lanes = lax.broadcasted_iota(jnp.int32, (total, HD), 1)
    turn_cos[...] = cos_part
    turn_sin[...] = jnp.where(lanes < HD // 2, -sin_part, sin_part)

    def turn(x):
        wide_x = x.astype(f32)
        return (wide_x * turn_cos[...] + pltpu.roll(wide_x, HD // 2, 1) * turn_sin[...]).astype(bf16)

    prefix_dev = pk_ref.shape[0]
    slot = lax.broadcasted_iota(jnp.int32, (1, prefix_dev), 1)
    prefix_seen = me * prefix_dev + slot < offset

    pool_dev = dk_ref.shape[0]
    block_dev = pool_dev // PAGE
    token = lax.broadcasted_iota(jnp.int32, (1, pool_dev), 1)
    block_of = me * block_dev + token // PAGE
    entry_of = jnp.zeros((count, pool_dev), jnp.int32)
    for k in range(BLK_ROW):
        entry_of = jnp.where(map_ref[:, k : k + 1] == block_of, k + 1, entry_of)
    place = (entry_of - 1) * PAGE + token % PAGE
    live = (entry_of > 0) & (place < lens)
    key_row = jnp.sum(jnp.where(live, row_ids + 1, 0), axis=0, keepdims=True) - 1

    nh = heads_at_once
    span_q = lax.broadcasted_iota(jnp.int32, (nh * count, 1), 0) % count
    own_j = lax.broadcasted_iota(jnp.int32, (1, count), 1)
    span_own = (own_j == me) & (own_j <= span_q)
    dec_q = lax.broadcasted_iota(jnp.int32, (nh * STEPS * count, 1), 0)
    dec_row = dec_q % count
    dec_step = (dec_q // count) % STEPS
    new_j = lax.broadcasted_iota(jnp.int32, (1, STEPS * count), 1)
    dec_own = (new_j % count == me) & (dec_row == me) & (new_j // count <= dec_step)
    pick = lax.broadcasted_iota(jnp.int32, (count, 1), 0) == me
    stat_lane = lax.broadcasted_iota(jnp.int32, (count, 2 * H), 1)
    stats[...] = jnp.zeros_like(stats)
    own_stats[...] = jnp.zeros_like(own_stats)
    across = (((1,), (1,)), ((), ()))

    def soft(q, keys, values, seen, keys2, values2, seen2):
        s1 = lax.dot_general(q, keys, across, preferred_element_type=f32) * scale
        s2 = lax.dot_general(q, keys2, across, preferred_element_type=f32) * scale
        s1 = jnp.where(seen, s1, neg_fill)
        s2 = jnp.where(seen2, s2, neg_fill)
        top = jnp.maximum(
            jnp.max(s1, axis=1, keepdims=True), jnp.max(s2, axis=1, keepdims=True)
        )
        top = jnp.maximum(top, top_floor)
        w1 = jnp.exp(s1 - top)
        w2 = jnp.exp(s2 - top)
        den = jnp.sum(w1, axis=1, keepdims=True) + jnp.sum(w2, axis=1, keepdims=True)
        num = jnp.dot(w1.astype(bf16), values, preferred_element_type=f32) + jnp.dot(
            w2.astype(bf16), values2, preferred_element_type=f32
        )
        return top, den, num

    kinds = 1 + STEPS

    def part_copy(i, g):
        peer = lax.rem(me + i, count)
        return pltpu.make_async_remote_copy(
            src_ref=own_parts.at[peer, g],
            dst_ref=parts.at[me, g],
            send_sem=send_sems.at[0, i],
            recv_sem=recv_sems.at[0, i],
            device_id={"tensor": peer},
            device_id_type=pl.DeviceIdType.MESH,
        )

    def all_parts(i):
        return pltpu.make_async_remote_copy(
            src_ref=own_parts.at[lax.rem(me + i, count)],
            dst_ref=parts.at[lax.rem(me + count - i, count)],
            send_sem=send_sems.at[0, i],
            recv_sem=recv_sems.at[0, i],
            device_id={"tensor": lax.rem(me + i, count)},
            device_id_type=pl.DeviceIdType.MESH,
        )

    def stat_copy(i):
        peer = lax.rem(me + i, count)
        return pltpu.make_async_remote_copy(
            src_ref=own_stats.at[pl.ds(pl.multiple_of(peer * 8, 8), 8)],
            dst_ref=all_stats.at[me],
            send_sem=send_sems.at[1, i],
            recv_sem=recv_sems.at[1, i],
            device_id={"tensor": peer},
            device_id_type=pl.DeviceIdType.MESH,
        )

    pl.semaphore_wait(pltpu.get_barrier_semaphore(), count - 1)

    def per_head(g, carry):
        cols = pl.ds(pl.multiple_of(g * HD, HD), HD)
        new_keys = turn(kv_head(g))
        new_values = kv_head(KVH + g)
        cache_ref[pl.ds(g, 1), :] = jnp.sum(
            jnp.where(pick, new_keys[:count].astype(f32), 0.0), axis=0, keepdims=True
        )
        cache_ref[pl.ds(KVH + g, 1), :] = jnp.sum(
            jnp.where(pick, new_values[:count].astype(f32), 0.0), axis=0, keepdims=True
        )
        for first in range(0, group, nh):
            turned = [turn(q_head(g * group + first + i)) for i in range(nh)]
            span_queries = jnp.concatenate([t[:count] for t in turned], axis=0)
            dec_queries = jnp.concatenate([t[count:] for t in turned], axis=0)
            span_top, span_den, span_num = soft(
                span_queries,
                pk_ref[:, cols],
                pv_ref[:, cols],
                prefix_seen,
                new_keys[:count],
                new_values[:count],
                span_own,
            )
            dec_top, dec_den, dec_num = soft(
                dec_queries,
                dk_ref[:, cols],
                dv_ref[:, cols],
                key_row == dec_row,
                new_keys[count:],
                new_values[count:],
                dec_own,
            )
            for i in range(nh):
                head = g * group + first + i
                for kind in range(1 + STEPS):
                    if kind == 0:
                        rows = slice(i * count, (i + 1) * count)
                        top, den, num = span_top[rows], span_den[rows], span_num[rows]
                    else:
                        at = (i * STEPS + kind - 1) * count
                        rows = slice(at, at + count)
                        top, den, num = dec_top[rows], dec_den[rows], dec_num[rows]
                    wide[pl.ds(kind * group + first + i, count, stride=kinds * group), :] = num
                    stats[kind] = jnp.where(
                        stat_lane == head,
                        top,
                        jnp.where(stat_lane == H + head, den, stats[kind]),
                    )

        def pack(d, carry):
            rows = pl.ds(pl.multiple_of(d * kinds * group, kinds * group), kinds * group)
            own_parts[d, g] = wide[rows, :].astype(bf16)
            return carry

        def send(i, carry):
            part_copy(i, g).start()
            return carry

        lax.fori_loop(0, count, pack, 0)
        lax.fori_loop(1, count, send, 0)
        return carry

    lax.fori_loop(0, KVH, per_head, 0)
    for kind in range(kinds):
        own_stats[pl.ds(kind, count, stride=8), :] = stats[kind]

    def send_stats(i, carry):
        stat_copy(i).start()
        return carry

    lax.fori_loop(1, count, send_stats, 0)
    own = (
        pltpu.make_async_copy(own_parts.at[me], parts.at[me], local_sems.at[0]),
        pltpu.make_async_copy(
            own_stats.at[pl.ds(pl.multiple_of(me * 8, 8), 8)], all_stats.at[me], local_sems.at[1]
        ),
    )
    for copy in own:
        copy.start()
    for j in range(2 * KVH):
        cache_out[0:1, j * HD : (j + 1) * HD] = cache_ref[j : j + 1, :].astype(cache_out.dtype)
    for copy in own:
        copy.wait()

    def finish(i, carry):
        all_parts(i).wait()
        stat_copy(i).wait()
        return carry

    lax.fori_loop(1, count, finish, 0)
    best = all_stats[0]
    for d in range(1, count):
        best = jnp.maximum(best, all_stats[d])
    den = jnp.zeros_like(best)
    for d in range(count):
        den = den + jnp.exp(all_stats[d] - best) * pltpu.roll(all_stats[d], H, 1)
    inverse = 1.0 / den
    share = jnp.concatenate(
        [jnp.exp(all_stats[d] - best) * inverse for d in range(count)], axis=0
    ).T
    sums = [jnp.zeros((H, HD), f32) for _ in range(kinds)]
    for d in range(count):
        arrived = parts[d].astype(f32)
        for kind in range(kinds):
            rows = arrived[:, kind * group : (kind + 1) * group, :].reshape(H, HD)
            sums[kind] = sums[kind] + share[:H, d * 8 + kind : d * 8 + kind + 1] * rows
    for h in range(H):
        cols = slice(h * HD, (h + 1) * HD)
        span_out[0:1, cols] = sums[0][h : h + 1, :].astype(span_out.dtype)
        for t in range(STEPS):
            decode_out[t : t + 1, cols] = sums[1 + t][h : h + 1, :].astype(decode_out.dtype)


def shards(
    layout,
    span_rows,
    decode_rows,
    norm_gain,
    w_query,
    w_keyval,
    prefix_keys,
    prefix_values,
    span_offset,
    pool_keys,
    pool_values,
    row_blocks,
    context_lens,
):
    count = lax.axis_size("tensor")
    span_dev = span_rows.shape[0]
    rows_dev = decode_rows.shape[1]
    assert span_dev == 1 and rows_dev == 1
    kinds = 1 + STEPS
    total = kinds * count
    cut, kv_cols = w_query.shape[1], w_keyval.shape[1]
    heads = front(layout, span_rows, decode_rows, norm_gain, w_query, w_keyval)
    if heads.ndim == 4:
        q_dev, kv_dev = cut // HD, kv_cols // HD
    else:
        heads = heads.transpose(1, 0, 2)
        heads = jnp.concatenate(
            [heads[:, :, :cut].reshape(total, -1, HD), heads[:, :, cut:].reshape(total, -1, HD)],
            axis=1,
        ).transpose(1, 0, 2)[None]
        q_dev, kv_dev = H, 2 * KVH
    cos_table, sin_table = rotation_tables(HD // 2)
    tile = lambda x: jnp.concatenate([x, x], axis=1)
    dma = pltpu.SemaphoreType.DMA
    span_attended, decode_attended, span_cache = pl.pallas_call(
        functools.partial(
            attend_kernel, count, H // KVH if count <= 32 else 1, (q_dev, kv_dev)
        ),
        out_shape=[
            jax.ShapeDtypeStruct((1, D), jnp.float32),
            jax.ShapeDtypeStruct((STEPS, D), jnp.float32),
            jax.ShapeDtypeStruct((1, 2 * KVH * HD), jnp.float32),
        ],
        in_specs=[VMEM_SPEC] * 6
        + [pl.BlockSpec(memory_space=pltpu.SMEM)] * 2
        + [VMEM_SPEC] * 2,
        out_specs=[VMEM_SPEC] * 3,
        scratch_shapes=[
            pltpu.VMEM((total, HD), jnp.float32),
            pltpu.VMEM((total, HD), jnp.float32),
            pltpu.VMEM((count * kinds * H // KVH, HD), jnp.float32),
            pltpu.VMEM((kinds, count, 2 * H), jnp.float32),
            pltpu.VMEM((2 * KVH, HD), jnp.float32),
            pltpu.VMEM((count, KVH, kinds * H // KVH, HD), jnp.bfloat16),
            pltpu.VMEM((count * 8, 2 * H), jnp.float32),
            pltpu.VMEM((count, KVH, kinds * H // KVH, HD), jnp.bfloat16),
            pltpu.VMEM((count, 8, 2 * H), jnp.float32),
            dma((2, count)),
            dma((2, count)),
            dma((2,)),
        ],
        compiler_params=pltpu.CompilerParams(
            collective_id=1, has_side_effects=True, vmem_limit_bytes=VMEM_BYTES
        ),
        name="attend",
    )(
        heads,
        prefix_keys,
        prefix_values,
        pool_keys.reshape(-1, KVH * HD),
        pool_values.reshape(-1, KVH * HD),
        row_blocks,
        span_offset,
        context_lens,
        tile(cos_table),
        tile(sin_table),
    )
    decode_attended = decode_attended.reshape(STEPS, 1, D)
    return tuple(x.astype(jnp.bfloat16) for x in (span_attended, decode_attended, span_cache))


def solution(mesh):
    in_specs = (
        P(("groups", "tensor"), None),
        P(None, ("groups", "tensor"), None),
        P(),
        P(None, "tensor"),
        P(None, "tensor"),
        P(("groups", "tensor"), None),
        P(("groups", "tensor"), None),
        P("groups"),
        P(("groups", "tensor"), None, None),
        P(("groups", "tensor"), None, None),
        P("groups", None),
        P("groups"),
    )
    out_specs = (
        P(("groups", "tensor"), None),
        P(None, ("groups", "tensor"), None),
        P(("groups", "tensor"), None),
    )
    return jax.shard_map(
        functools.partial(shards, layout_of(mesh)),
        mesh=mesh,
        in_specs=in_specs,
        out_specs=out_specs,
        check_vma=False,
    )
```
